32 devices in a mesh: wide: 8 (over y, x, core), tensor: 4 (over z).
Axes of the slice: x: 2, y: 2, z: 4, core: 2. Of those that a mesh axis runs over, the one named last changes fastest.
Arguments:
- layer_input: bfloat16 [8192, 2048], P(('wide', 'tensor')), may hold values from -6 to 6
- lengths: int32 [8, 4], P('wide'), may hold values from 1 to 192, 512 in all within a row
- gain_attn: float32 [2048], P(('wide', 'tensor')), may hold values from 0.25 to 1.75
- w_query: float32 [2048, 2048], P('wide', 'tensor'), may hold values from -0.125 to 0.125
- w_key: float32 [2048, 1024], P('wide', 'tensor'), may hold values from -0.125 to 0.125
- w_value: float32 [2048, 1024], P('wide', 'tensor'), may hold values from -0.125 to 0.125
- w_out: float32 [2048, 2048], P('tensor', 'wide'), may hold values from -1 to 1
- gain_ffn: float32 [2048], P(('wide', 'tensor')), may hold values from 0.25 to 1.75
- w_gate: float32 [2048, 8192], P('wide', 'tensor'), may hold values from -0.125 to 0.125
- w_up: float32 [2048, 8192], P('wide', 'tensor'), may hold values from -0.125 to 0.125
- w_down: float32 [8192, 2048], P('tensor', 'wide'), may hold values from -0.0625 to 0.0625
- cotangent: bfloat16 [8192, 2048], P(('wide', 'tensor')), may hold values from -6 to 6
Outputs:
- output: bfloat16 [8192, 2048], P(('wide', 'tensor'))
- input_grad: bfloat16 [8192, 2048], P(('wide', 'tensor'))
- grad_gain_attn: float32 [2048], P(('wide', 'tensor'))
- grad_query: float32 [2048, 2048], P('wide', 'tensor')
- grad_key: float32 [2048, 1024], P('wide', 'tensor')
- grad_value: float32 [2048, 1024], P('wide', 'tensor')
- grad_out: float32 [2048, 2048], P('tensor', 'wide')
- grad_gain_ffn: float32 [2048], P(('wide', 'tensor'))
- grad_gate: float32 [2048, 8192], P('wide', 'tensor')
- grad_up: float32 [2048, 8192], P('wide', 'tensor')
- grad_down: float32 [8192, 2048], P('tensor', 'wide')
The draws below stay inside these ranges and needn't reach their ends.
Inputs may be any that keep to these rules, and one draw needn't show every extreme that they name: Each row of lengths sums to 512, and its largest entry is 192.
All inputs are finite; a program needn't handle non-finite values.
Results may differ from the reference program's by a relative error of at most 0.023.
Values may be sent and summed in bfloat16 or wider, within the bound.
No kernel may reach another device: no remote copies, remote signals or barrier semaphores. Data moves between devices by JAX's collectives and lax.ppermute only.
A program may use at most 192 MiB of HBM per device.

```python
import math
import jax
import jax.numpy as jnp
import numpy as np
from jax import lax

D = 2048
HEADS = 16
KV_HEADS = 8
HEAD_DIM = 128
FF = 8192
CONT = 128
PROMPT_W = 512
ROWS = 1024
CONTS_W = 4
CONT_MOST = 192
TOKENS = 8192
N_WIDE = 8


def levels(rng, dims, shards, smallest, top_value):
    def one(dim, blocks):
        draws = jax.random.uniform(jax.random.fold_in(jax.random.fold_in(rng, 6), dim), (blocks,), jnp.float32, smallest / len(shards), top_value / len(shards))
        return jnp.repeat(jnp.exp(draws), dims[dim] // blocks).reshape((-1,) + (1,) * (len(dims) - dim - 1))

    gain = one(*shards[0])
    for cut in shards[1:]:
        gain = gain * one(*cut)
    return gain


def split_up(amount, total, reach, slope):
    weights = [(1 << 20) // math.isqrt(grade ** slope) + 1 for grade in range(2, amount + 1)]
    surplus, counts = total - reach - (amount - 1), [1] * (amount - 1)
    while surplus > 0:
        free = [i for i in range(amount - 1) if counts[i] < reach]
        whole, left = sum([weights[i] for i in free]), surplus
        for i in free:
            addition = min(reach - counts[i], max(1, left * weights[i] // whole), surplus)
            counts[i] = counts[i] + addition
            surplus = surplus - addition
    return np.array([reach] + counts)


def uneven_parts(own_key, amount, total, reach, slope):
    if amount == 2:
        one = jax.random.randint(own_key, (), max(1, total - reach), min(reach, total - 1) + 1)
        return jnp.stack([one, total - one])
    sizes = jnp.asarray(split_up(amount, total, reach, slope), jnp.int32)
    twos = (amount - 1) // 2
    donor, taker = sizes[1:1 + 2 * twos:2], sizes[2:2 + 2 * twos:2]
    margin = jnp.minimum(donor - 1, reach - taker)
    moved = jax.random.randint(jax.random.fold_in(own_key, 1), (twos,), 0, 1 << 20) % (margin + 1)
    sizes = sizes.at[1:1 + 2 * twos:2].set(donor - moved).at[2:2 + 2 * twos:2].set(taker + moved)
    return sizes[jax.random.permutation(jax.random.fold_in(own_key, 2), amount)]


def gaussian(rng, extent, width, limit, pieces=(), held_as=jnp.bfloat16):
    loudness = levels(rng, extent, pieces, -0.22, 0.18) if pieces else 1.0
    drawn = jax.random.normal(rng, extent, jnp.float32) * width * loudness
    return jnp.minimum(jnp.maximum(drawn, -limit), limit).astype(held_as)


def setup_inputs(seed: int = 0) -> dict:
    streams_of = jax.random.split(jax.random.key(seed), 13)
    return {
        "layer_input": gaussian(streams_of[0], (TOKENS, D), 1.0, 6.0, ((0, 32),)),
        "lengths": jax.vmap(lambda own: uneven_parts(own, CONTS_W, CONTS_W * CONT, CONT_MOST, 0))(jax.random.split(streams_of[1], N_WIDE)).reshape((N_WIDE, CONTS_W)).astype(jnp.int32),
        "gain_attn": jnp.clip(1.0 + 0.15 * jax.random.normal(streams_of[2], (D,), jnp.float32), 0.25, 1.75),
        "w_query": gaussian(streams_of[3], (D, HEADS * HEAD_DIM), D ** -0.5, 0.125, ((0, 8), (1, 4)), jnp.float32),
        "w_key": gaussian(streams_of[4], (D, KV_HEADS * HEAD_DIM), D ** -0.5, 0.125, ((0, 8), (1, 4)), jnp.float32),
        "w_value": gaussian(streams_of[5], (D, KV_HEADS * HEAD_DIM), D ** -0.5, 0.125, ((0, 8), (1, 4)), jnp.float32),
        "w_out": gaussian(streams_of[6], (HEADS * HEAD_DIM, D), (max(HEADS * HEAD_DIM // 64, 4)) ** -0.5, 1.0, ((0, 4), (1, 8)), jnp.float32),
        "gain_ffn": jnp.clip(1.0 + 0.15 * jax.random.normal(streams_of[7], (D,), jnp.float32), 0.25, 1.75),
        "w_gate": gaussian(streams_of[8], (D, FF), D ** -0.5, 0.125, ((0, 8), (1, 4)), jnp.float32),
        "w_up": gaussian(streams_of[9], (D, FF), D ** -0.5, 0.125, ((0, 8), (1, 4)), jnp.float32),
        "w_down": gaussian(streams_of[10], (FF, D), FF ** -0.5, 0.0625, ((0, 4), (1, 8)), jnp.float32),
        "cotangent": gaussian(streams_of[11], (TOKENS, D), 1.0, 6.0, ((0, 32),)),
    }


@jax.custom_vjp
def low(v):
    return lax.optimization_barrier(v.astype(jnp.bfloat16)).astype(jnp.float32)

@jax.custom_vjp
def low_back(v):
    return v

def low_keep(v):
    return (low(v), None)

def low_pass(kept, grad):
    return (grad,)

def back_keep(v):
    return (v, None)

def back_low(kept, grad):
    return (low(grad),)
low.defvjp(low_keep, low_pass)
low_back.defvjp(back_keep, back_low)
norm_eps = 1e-05
rope_base = 1000000.0
masked_score = -1e+30
highest = lax.Precision.HIGHEST

def normed(values):
    return values * lax.rsqrt(lax.optimization_barrier(jnp.mean(values * values, axis=-1, keepdims=True)) + norm_eps)

def layout(lengths_row, half_index, row_count, prompt_rows):
    cont_count = lengths_row.shape[0]
    ends_at = jnp.cumsum(lengths_row).astype(jnp.int32)
    starts_at = (ends_at - lengths_row).astype(jnp.int32)
    offsets = jnp.arange(row_count - prompt_rows, dtype=jnp.int32)
    which_cont = lax.optimization_barrier(jnp.sum((offsets[:, None] >= ends_at[None, :]).astype(jnp.int32), axis=1)).astype(jnp.int32)
    picked = (which_cont[:, None] == jnp.arange(cont_count, dtype=jnp.int32)[None, :]).astype(jnp.int32)
    begins = lax.optimization_barrier(jnp.sum(picked * starts_at[None, :], axis=1)).astype(jnp.int32)
    prompt_pos = (half_index * prompt_rows + jnp.arange(prompt_rows, dtype=jnp.int32)).astype(jnp.int32)
    cont_pos = (2 * prompt_rows + offsets - begins).astype(jnp.int32)
    segment = jnp.concatenate([jnp.zeros((prompt_rows,), jnp.int32), (which_cont + 1).astype(jnp.int32)])
    position = jnp.concatenate([prompt_pos, cont_pos])
    return (segment, position)

def rope_tables(position):
    half_dim = HEAD_DIM // 2
    inverse = rope_base ** (-jnp.arange(half_dim, dtype=jnp.float32) * (2.0 / HEAD_DIM))
    angles = position.astype(jnp.float32)[:, None] * inverse[None, :]
    cosine = jnp.cos(angles)
    sine_part = jnp.sin(angles)
    return (jnp.concatenate([cosine, cosine], 1), jnp.concatenate([sine_part, sine_part], 1))

def rotate(values, cosine, sine_part):
    half_dim = values.shape[-1] // 2
    turned = jnp.concatenate([-values[..., half_dim:], values[..., :half_dim]], -1)
    return values * cosine[:, None, :] + turned * sine_part[:, None, :]

def attend(query_rot, key_all, value_all, segment, position, key_segment, key_position):
    row_count = query_rot.shape[0]
    block_rows = min(512, row_count)
    block_count = row_count // block_rows
    group_size = HEADS // KV_HEADS
    score_scale = HEAD_DIM ** (-0.5)

    def one_block(inputs):
        query_block, seg_block, pos_block = inputs
        grouped = query_block.reshape(block_rows, KV_HEADS, group_size, HEAD_DIM)
        raw_scores = low_back(jnp.einsum('bkgd,nkd->kgbn', grouped, key_all, precision=highest))
        scores = raw_scores * score_scale
        allowed = ((key_segment[None, :] == 0) | (key_segment[None, :] == seg_block[:, None])) & (key_position[None, :] <= pos_block[:, None])
        scores = jnp.where(allowed[None, None], scores, masked_score)
        shifted = scores - lax.optimization_barrier(jnp.max(scores, axis=-1, keepdims=True))
        weights_exp = jnp.exp(shifted)
        probs = weights_exp / lax.optimization_barrier(jnp.sum(weights_exp, axis=-1, keepdims=True))
        attended = jnp.einsum('kgbn,nkd->bkgd', low(probs), value_all, precision=highest)
        return attended.reshape(block_rows, HEADS * HEAD_DIM)
    results = lax.map(jax.checkpoint(one_block), (query_rot.reshape(block_count, block_rows, HEADS, HEAD_DIM), segment.reshape(block_count, block_rows), position.reshape(block_count, block_rows)))
    return results.reshape(row_count, HEADS * HEAD_DIM)

def group_layer(x_group, lengths_pair, gain_attn, w_query, w_key, w_value, w_out, gain_ffn, w_gate, w_up, w_down):
    h_one = low(normed(x_group) * gain_attn)
    query_raw = low_back(jnp.dot(h_one, w_query, precision=highest))
    key_raw = low_back(jnp.dot(h_one, w_key, precision=highest))
    value_low = low(low_back(jnp.dot(h_one, w_value, precision=highest)))
    rotated_q = []
    rotated_k = []
    metas = []
    for half_index in range(2):
        segment, position = layout(lengths_pair[half_index], half_index, ROWS, PROMPT_W)
        cosine, sine_part = rope_tables(position)
        first_row = half_index * ROWS
        rotated_q.append(low(rotate(query_raw[first_row:first_row + ROWS].reshape(ROWS, HEADS, HEAD_DIM), cosine, sine_part)))
        rotated_k.append(low(rotate(key_raw[first_row:first_row + ROWS].reshape(ROWS, KV_HEADS, HEAD_DIM), cosine, sine_part)))
        metas.append((segment, position))
    value_rows = value_low.reshape(2 * ROWS, KV_HEADS, HEAD_DIM)
    attended_parts = []
    for half_index in range(2):
        other_half = 1 - half_index
        key_all = jnp.concatenate([rotated_k[other_half][:PROMPT_W], rotated_k[half_index]], 0)
        value_all = jnp.concatenate([value_rows[other_half * ROWS:other_half * ROWS + PROMPT_W], value_rows[half_index * ROWS:(half_index + 1) * ROWS]], 0)
        key_segment = jnp.concatenate([jnp.zeros((PROMPT_W,), jnp.int32), metas[half_index][0]])
        key_position = jnp.concatenate([metas[other_half][1][:PROMPT_W], metas[half_index][1]])
        attended_parts.append(attend(rotated_q[half_index], key_all, value_all, metas[half_index][0], metas[half_index][1], key_segment, key_position))
    attended = low(low_back(jnp.concatenate(attended_parts, 0)))
    x_mid = x_group + low_back(jnp.dot(attended, w_out, precision=highest))
    h_two = low(normed(x_mid) * gain_ffn)
    gate_val = low_back(jnp.dot(h_two, w_gate, precision=highest))
    up_val = low_back(jnp.dot(h_two, w_up, precision=highest))
    hidden = low(gate_val * jax.nn.sigmoid(gate_val) * up_val)
    return x_mid + low_back(jnp.dot(hidden, w_down, precision=highest))

def forward(x_float, lengths, gain_attn, w_query, w_key, w_value, w_out, gain_ffn, w_gate, w_up, w_down):
    query_low = low(w_query)
    key_low = low(w_key)
    value_wlow = low(w_value)
    out_low = low(w_out)
    gate_low = low(w_gate)
    up_low = low(w_up)
    down_low = low(w_down)
    group_count = N_WIDE // 2
    x_groups = x_float.reshape(group_count, 2 * ROWS, D)
    length_groups = lengths.reshape(group_count, 2, CONTS_W)

    def step_group(carried, inputs):
        x_group, lengths_pair = inputs
        result = group_layer(x_group, lengths_pair, gain_attn, query_low, key_low, value_wlow, out_low, gain_ffn, gate_low, up_low, down_low)
        return (carried, result)
    _, results = lax.scan(jax.checkpoint(step_group), jnp.zeros((), jnp.float32), (x_groups, length_groups))
    return results.reshape(N_WIDE * ROWS, D)

def reference(layer_input, lengths, gain_attn, w_query, w_key, w_value, w_out, gain_ffn, w_gate, w_up, w_down, cotangent):

    def wrapped(x_float, gain_one, query_w, key_w, value_w, out_w, gain_two, gate_w, up_w, down_w):
        return forward(x_float, lengths, gain_one, query_w, key_w, value_w, out_w, gain_two, gate_w, up_w, down_w)
    result, pullback = jax.vjp(wrapped, layer_input.astype(jnp.float32), gain_attn, w_query, w_key, w_value, w_out, gain_ffn, w_gate, w_up, w_down)
    grads = pullback(cotangent.astype(jnp.float32))
    return (result.astype(jnp.bfloat16), grads[0].astype(jnp.bfloat16), grads[1], grads[2], grads[3], grads[4], grads[5], grads[6], grads[7], grads[8], grads[9])
```

```python
import jax
import jax.numpy as jnp
from jax import lax
from jax.sharding import PartitionSpec as P

HEAD_DIM = 128
PROMPT = 1024


norm_eps = 1e-05
rope_base = 1000000.0
masked_score = -1e30


def swapped(block, axis, apart):
    count = lax.axis_size(axis)
    route = []
    for low in range(count):
        high = low | 1 << apart
        if high != low and high < count:
            route += [(low, high), (high, low)]
    return lax.ppermute(block, axis, route)


def layout(lengths_row, half_index, row_count, prompt_rows):
    cont_count = lengths_row.shape[0]
    ends_at = jnp.cumsum(lengths_row)
    starts_at = ends_at - lengths_row
    offsets = jnp.arange(row_count - prompt_rows, dtype=jnp.int32)
    which_cont = jnp.sum((offsets[:, None] >= ends_at[None, :]).astype(jnp.int32), axis=1)
    picked = (which_cont[:, None] == jnp.arange(cont_count, dtype=jnp.int32)[None, :]).astype(
        jnp.int32
    )
    begins = jnp.sum(picked * starts_at[None, :], axis=1)
    prompt_pos = half_index * prompt_rows + jnp.arange(prompt_rows, dtype=jnp.int32)
    cont_pos = 2 * prompt_rows + offsets - begins
    segment = jnp.concatenate([jnp.zeros((prompt_rows,), jnp.int32), which_cont + 1])
    position = jnp.concatenate([prompt_pos, cont_pos])
    return (segment, position)


def rope_tables(position, head_dim):
    half_dim = head_dim // 2
    inverse = rope_base ** (-jnp.arange(half_dim, dtype=jnp.float32) * (2.0 / head_dim))
    angles = position.astype(jnp.float32)[:, None] * inverse[None, :]
    cosine = jnp.cos(angles)
    sine_part = jnp.sin(angles)
    return (jnp.concatenate([cosine, cosine], 1), jnp.concatenate([sine_part, sine_part], 1))


def rotate(values, cosine, sine_part):
    half_dim = values.shape[-1] // 2
    turned = jnp.concatenate([-values[..., half_dim:], values[..., :half_dim]], -1)
    return values * cosine[:, None, :] + turned * sine_part[:, None, :]


def unrotate(grads, cosine, sine_part):
    half_dim = grads.shape[-1] // 2
    scaled = grads * sine_part[:, None, :]
    turned = jnp.concatenate([-scaled[..., half_dim:], scaled[..., :half_dim]], -1)
    return grads * cosine[:, None, :] - turned


def dot_rows(left, right):
    return lax.dot_general(
        left, right, (((0,), (0,)), ((), ())), preferred_element_type=jnp.float32
    )


def dot_back(left, right):
    return lax.dot_general(
        left, right, (((1,), (1,)), ((), ())), preferred_element_type=jnp.float32
    )


def meeting(bit, stride, count):
    return [(low, low ^ (bit * stride)) for low in range(count)]


class Square:
    def __init__(self, axis, stride):
        self.axis = axis
        self.stride = stride
        self.count = lax.axis_size(axis)
        self.place = lax.axis_index(axis) // stride % 4

    def meet(self, block, bit):
        return lax.ppermute(block, self.axis, meeting(bit, self.stride, self.count))

    def gather(self, own):
        first = self.meet(own, 1)
        second = self.meet(own, 2)
        cut = own.shape[0] // 2
        if cut == 0:
            return [own, first, second, self.meet(second, 1)]
        low_part = self.meet(second[:cut], 1)
        high_part = self.meet(first[cut:], 2)
        return [own, first, second, jnp.concatenate([low_part, high_part], 0)]

    def scatter(self, term_of):
        sent = jnp.bfloat16
        far = term_of(3).astype(sent)
        cut = far.shape[0] // 2
        low_part = self.meet(far[:cut], 1)
        high_part = self.meet(far[cut:], 2)
        first = term_of(1)
        second = term_of(2)
        first = jnp.concatenate([first[:cut], first[cut:] + high_part], 0).astype(sent)
        second = jnp.concatenate([second[:cut] + low_part, second[cut:]], 0).astype(sent)
        from_first = self.meet(first, 1)
        from_second = self.meet(second, 2)
        return term_of(0) + from_first.astype(jnp.float32) + from_second.astype(jnp.float32)

    def scatter_small(self, terms):
        def pick(j):
            return lax.dynamic_index_in_dim(terms, self.place ^ j, 0, keepdims=False)

        passed = pick(2) + self.meet(pick(3), 1)
        return pick(0) + self.meet(pick(1), 1) + self.meet(passed, 2)

    def ordered(self, slots, axis):
        extent = slots[0].shape[axis]
        shape = list(slots[0].shape)
        shape[axis] = 4 * extent
        whole = jnp.zeros(shape, slots[0].dtype)
        for j in range(4):
            whole = lax.dynamic_update_slice_in_dim(
                whole, slots[j], (self.place ^ j) * extent, axis
            )
        return whole


def twin(block):
    return lax.ppermute(block, "wide", meeting(1, 1, lax.axis_size("wide")))


def custom_mesh():
    return lax.axis_size("wide") == 8 and lax.axis_size("tensor") == 4


def wide_gather(own, axis):
    if not custom_mesh():
        return lax.all_gather(own, "wide", axis=axis, tiled=True)
    square = Square("wide", 2)
    core = lax.axis_index("wide") % 2
    slots = square.gather(own)
    extent = own.shape[axis]
    shape = list(own.shape)
    shape[axis] = 8 * extent
    whole = jnp.zeros(shape, own.dtype)
    for j in range(4):
        pair = (square.place ^ j) * 2
        whole = lax.dynamic_update_slice_in_dim(whole, slots[j], (pair + core) * extent, axis)
        whole = lax.dynamic_update_slice_in_dim(
            whole, twin(slots[j]), (pair + 1 - core) * extent, axis
        )
    return whole


def wide_scatter(grad, axis):
    if not custom_mesh():
        return lax.psum_scatter(
            grad.astype(jnp.bfloat16), "wide", scatter_dimension=axis, tiled=True
        ).astype(jnp.float32)
    square = Square("wide", 2)
    core = lax.axis_index("wide") % 2
    extent = grad.shape[axis] // 8
    grad_low = grad.astype(jnp.bfloat16)

    def term_of(j):
        pair = (square.place ^ j) * 2
        other = lax.dynamic_slice_in_dim(grad_low, (pair + 1 - core) * extent, extent, axis)
        mine = lax.dynamic_slice_in_dim(grad_low, (pair + core) * extent, extent, axis)
        return mine.astype(jnp.float32) + twin(other).astype(jnp.float32)

    return square.scatter(term_of)


def rows_gather(values):
    if not custom_mesh():
        return lax.all_gather(values, "tensor", axis=0, tiled=True)
    square = Square("tensor", 1)
    return square.ordered(square.gather(values), 0)


def rows_scatter(term_fn, local_rows):
    if not custom_mesh():
        return lax.psum_scatter(
            term_fn(jnp.int32(0), local_rows * lax.axis_size("tensor")).astype(jnp.bfloat16),
            "tensor",
            scatter_dimension=0,
            tiled=True,
        ).astype(jnp.float32)
    square = Square("tensor", 1)
    return square.scatter(lambda j: term_fn((square.place ^ j) * local_rows, local_rows))


def gains_gather(gains):
    if not custom_mesh():
        return lax.all_gather(gains, ("wide", "tensor"), axis=1, tiled=True)
    own = gains[None]
    tensor_square = Square("tensor", 1)
    chip_square = Square("wide", 2)
    core = lax.axis_index("wide") % 2
    lanes = tensor_square.ordered(tensor_square.gather(own), 0)[None, None]
    other = twin(lanes)
    pair = jnp.where(
        core == 0, jnp.concatenate([lanes, other], 1), jnp.concatenate([other, lanes], 1)
    )
    whole = chip_square.ordered(chip_square.gather(pair), 0)
    return jnp.moveaxis(whole, 3, 0).reshape(gains.shape[0], -1)


def gain_scatter(part):
    if not custom_mesh():
        return lax.psum_scatter(part, ("wide", "tensor"), scatter_dimension=0, tiled=True)
    core = lax.axis_index("wide") % 2
    terms = part.reshape(4, 2, 4, -1)
    mine = lax.dynamic_index_in_dim(terms, core, 1, keepdims=False)
    other = lax.dynamic_index_in_dim(terms, 1 - core, 1, keepdims=False)
    chip_terms = Square("wide", 2).scatter_small(mine + twin(other))
    return Square("tensor", 1).scatter_small(chip_terms)


def rows_of(values, first_row, num_rows):
    return lax.dynamic_slice_in_dim(values, first_row, num_rows, 0)


def masked_scores(grouped, key_all, seg_block, pos_block, key_segment, key_position, score_scale):
    scores = (
        jnp.einsum("bkgd,nkd->kgbn", grouped, key_all, preferred_element_type=jnp.float32)
        * score_scale
    )
    allowed = ((key_segment[None, :] == 0) | (key_segment[None, :] == seg_block[:, None])) & (
        key_position[None, :] <= pos_block[:, None]
    )
    return jnp.where(allowed[None, None], scores, masked_score)


def on_device(
    layer_input,
    lengths,
    gain_attn,
    w_query,
    w_key,
    w_value,
    w_out,
    gain_ffn,
    w_gate,
    w_up,
    w_down,
    cotangent,
):
    tensor_count = lax.axis_size("tensor")
    local_rows = layer_input.shape[0]
    row_count = local_rows * tensor_count
    prompt_rows = PROMPT // 2
    head_dim = HEAD_DIM
    query_heads = w_query.shape[1] // head_dim
    kv_heads = w_key.shape[1] // head_dim
    group_size = query_heads // kv_heads
    score_scale = head_dim ** (-0.5)
    block_rows = min(512, row_count)
    block_count = row_count // block_rows
    half_index = lax.axis_index("wide") % 2
    low_type = jnp.bfloat16
    query_cols, kv_cols = w_query.shape[1], w_key.shape[1]
    hidden_cols = w_gate.shape[1]
    gains = gains_gather(jnp.stack([gain_attn, gain_ffn]))
    gain_one, gain_two = gains[0], gains[1]
    x_low_all = rows_gather(layer_input)
    qkv_wide = wide_gather(
        jnp.concatenate(
            [w_query.astype(low_type), w_key.astype(low_type), w_value.astype(low_type)], 1
        ),
        0,
    )
    o_wide = wide_gather(w_out.astype(low_type), 1)
    gate_up_wide = wide_gather(
        jnp.concatenate([w_gate.astype(low_type), w_up.astype(low_type)], 1), 0
    )
    down_wide = wide_gather(w_down.astype(low_type), 1)
    x_float = layer_input.astype(jnp.float32)
    inv_one = lax.rsqrt(jnp.mean(x_float * x_float, axis=-1, keepdims=True) + norm_eps)
    normed_one = x_float * inv_one
    x_all = x_low_all.astype(jnp.float32)
    normed_all = x_all * lax.rsqrt(jnp.mean(x_all * x_all, axis=-1, keepdims=True) + norm_eps)
    h_one_all = (normed_all * gain_one).astype(jnp.bfloat16)
    qkv_raw = jnp.dot(h_one_all, qkv_wide, preferred_element_type=jnp.float32)
    query_raw = qkv_raw[:, :query_cols]
    key_raw = qkv_raw[:, query_cols : query_cols + kv_cols]
    value_raw = qkv_raw[:, query_cols + kv_cols :]
    segment, position = layout(lengths[0], half_index, row_count, prompt_rows)
    cosine, sine_part = rope_tables(position, head_dim)
    query_rot = rotate(
        query_raw.reshape(row_count, query_heads, head_dim), cosine, sine_part
    ).astype(jnp.bfloat16)
    key_rot = rotate(key_raw.reshape(row_count, kv_heads, head_dim), cosine, sine_part).astype(
        jnp.bfloat16
    )
    value_low = value_raw.astype(jnp.bfloat16).reshape(row_count, kv_heads, head_dim)
    far_key, far_value = swapped((key_rot[:prompt_rows], value_low[:prompt_rows]), "wide", 0)
    key_all = jnp.concatenate([far_key, key_rot], 0)
    value_all = jnp.concatenate([far_value, value_low], 0)
    far_position = (1 - half_index) * prompt_rows + jnp.arange(prompt_rows, dtype=jnp.int32)
    key_segment = jnp.concatenate([jnp.zeros((prompt_rows,), jnp.int32), segment])
    key_position = jnp.concatenate([far_position, position])
    query_blocks = query_rot.reshape(block_count, block_rows, query_heads, head_dim)
    seg_blocks = segment.reshape(block_count, block_rows)
    pos_blocks = position.reshape(block_count, block_rows)

    def forward_block(inputs):
        query_block, seg_block, pos_block = inputs
        grouped = query_block.reshape(block_rows, kv_heads, group_size, head_dim)
        scores = masked_scores(
            grouped, key_all, seg_block, pos_block, key_segment, key_position, score_scale
        )
        row_top = jnp.max(scores, axis=-1, keepdims=True)
        weights_exp = jnp.exp(scores - row_top)
        row_total = jnp.sum(weights_exp, axis=-1, keepdims=True)
        probs_low = (weights_exp / row_total).astype(jnp.bfloat16)
        attended = jnp.einsum(
            "kgbn,nkd->bkgd", probs_low, value_all, preferred_element_type=jnp.float32
        )
        log_total = (row_top + jnp.log(row_total))[..., 0]
        return (
            attended.reshape(block_rows, query_heads * head_dim).astype(jnp.bfloat16),
            log_total,
        )

    attn_blocks, log_blocks = lax.map(forward_block, (query_blocks, seg_blocks, pos_blocks))
    attn_low = attn_blocks.reshape(row_count, query_heads * head_dim)

    def attn_term(first_row, num_rows):
        return jnp.dot(rows_of(attn_low, first_row, num_rows), o_wide, preferred_element_type=jnp.float32)

    x_mid = x_float + rows_scatter(attn_term, local_rows)
    inv_two = lax.rsqrt(jnp.mean(x_mid * x_mid, axis=-1, keepdims=True) + norm_eps)
    normed_two = x_mid * inv_two
    h_two = (normed_two * gain_two).astype(jnp.bfloat16)
    h_two_all = rows_gather(h_two)
    gate_up_val = jnp.dot(h_two_all, gate_up_wide, preferred_element_type=jnp.float32)
    gate_val = gate_up_val[:, :hidden_cols]
    up_val = gate_up_val[:, hidden_cols:]
    gate_sig = jax.nn.sigmoid(gate_val)
    hidden_low = (gate_val * gate_sig * up_val).astype(jnp.bfloat16)

    def ffn_term(first_row, num_rows):
        return jnp.dot(rows_of(hidden_low, first_row, num_rows), down_wide, preferred_element_type=jnp.float32)

    output = (x_mid + rows_scatter(ffn_term, local_rows)).astype(jnp.bfloat16)
    cot_float = cotangent.astype(jnp.float32)
    cot_all = rows_gather(cotangent)
    d_hidden = dot_back(cot_all, down_wide)
    grad_down = dot_rows(hidden_low, cot_all)
    d_up = (d_hidden * gate_val * gate_sig).astype(jnp.bfloat16)
    d_gate = (d_hidden * up_val * gate_sig * (1.0 + gate_val * (1.0 - gate_sig))).astype(
        jnp.bfloat16
    )
    d_gate_up = jnp.concatenate([d_gate, d_up], 1)

    def ffn_back_term(first_row, num_rows):
        return dot_back(rows_of(d_gate_up, first_row, num_rows), gate_up_wide)

    d_h_two = rows_scatter(ffn_back_term, local_rows)
    grad_gate_up = dot_rows(h_two_all, d_gate_up)
    gain_two_part = jnp.sum(d_h_two * normed_two, axis=0)
    e_two = d_h_two * gain_two
    d_mid = cot_float + inv_two * (
        e_two - normed_two * jnp.mean(e_two * normed_two, axis=-1, keepdims=True)
    )
    d_mid_all = rows_gather(d_mid.astype(jnp.bfloat16))
    grad_out = dot_rows(attn_low, d_mid_all)
    d_attended = dot_back(d_mid_all, o_wide).astype(jnp.bfloat16)
    d_blocks = d_attended.reshape(block_count, block_rows, query_heads, head_dim)

    def backward_block(carried, inputs):
        key_grad, value_grad = carried
        query_block, d_block, log_total, seg_block, pos_block = inputs
        grouped = query_block.reshape(block_rows, kv_heads, group_size, head_dim)
        d_grouped = d_block.reshape(block_rows, kv_heads, group_size, head_dim)
        scores = masked_scores(
            grouped, key_all, seg_block, pos_block, key_segment, key_position, score_scale
        )
        probs = jnp.exp(scores - log_total[..., None])
        probs_low = probs.astype(jnp.bfloat16)
        d_probs = jnp.einsum(
            "bkgd,nkd->kgbn", d_grouped, value_all, preferred_element_type=jnp.float32
        )
        row_term = jnp.sum(probs * d_probs, axis=-1, keepdims=True)
        d_scores = (probs * (d_probs - row_term) * score_scale).astype(jnp.bfloat16)
        d_query = jnp.einsum(
            "kgbn,nkd->bkgd", d_scores, key_all, preferred_element_type=jnp.float32
        )
        key_grad = key_grad + jnp.einsum(
            "kgbn,bkgd->nkd", d_scores, grouped, preferred_element_type=jnp.float32
        )
        value_grad = value_grad + jnp.einsum(
            "kgbn,bkgd->nkd", probs_low, d_grouped, preferred_element_type=jnp.float32
        )
        return ((key_grad, value_grad), d_query.reshape(block_rows, query_heads, head_dim))

    zero_grad = jnp.zeros((prompt_rows + row_count, kv_heads, head_dim), jnp.float32)
    (key_grad, value_grad), d_query_blocks = lax.scan(
        backward_block,
        (zero_grad, zero_grad),
        (query_blocks, d_blocks, log_blocks, seg_blocks, pos_blocks),
    )
    far_key_grad, far_value_grad = (
        swapped(key_grad[:prompt_rows].astype(jnp.bfloat16), "wide", 0).astype(jnp.float32),
        swapped(value_grad[:prompt_rows].astype(jnp.bfloat16), "wide", 0).astype(jnp.float32),
    )
    own_key_grad = jnp.concatenate(
        [key_grad[prompt_rows : 2 * prompt_rows] + far_key_grad, key_grad[2 * prompt_rows :]], 0
    )
    own_value_grad = jnp.concatenate(
        [value_grad[prompt_rows : 2 * prompt_rows] + far_value_grad, value_grad[2 * prompt_rows :]],
        0,
    )
    d_query_rot = d_query_blocks.reshape(row_count, query_heads, head_dim)
    d_query_low = (
        unrotate(d_query_rot, cosine, sine_part)
        .reshape(row_count, query_heads * head_dim)
        .astype(jnp.bfloat16)
    )
    d_key_low = (
        unrotate(own_key_grad, cosine, sine_part)
        .reshape(row_count, kv_heads * head_dim)
        .astype(jnp.bfloat16)
    )
    d_value_low = own_value_grad.reshape(row_count, kv_heads * head_dim).astype(jnp.bfloat16)
    d_qkv_low = jnp.concatenate([d_query_low, d_key_low, d_value_low], 1)
    grad_qkv = dot_rows(h_one_all, d_qkv_low)

    def attn_back_term(first_row, num_rows):
        return dot_back(rows_of(d_qkv_low, first_row, num_rows), qkv_wide)

    d_h_one = rows_scatter(attn_back_term, local_rows)
    gain_one_part = jnp.sum(d_h_one * normed_one, axis=0)
    e_one = d_h_one * gain_one
    input_grad = (
        d_mid
        + inv_one * (e_one - normed_one * jnp.mean(e_one * normed_one, axis=-1, keepdims=True))
    ).astype(jnp.bfloat16)
    grad_down = wide_scatter(grad_down, 1)
    grad_gate_up = wide_scatter(grad_gate_up, 0)
    grad_out = wide_scatter(grad_out, 1)
    grad_qkv = wide_scatter(grad_qkv, 0)
    grad_gate, grad_up = grad_gate_up[:, :hidden_cols], grad_gate_up[:, hidden_cols:]
    grad_query = grad_qkv[:, :query_cols]
    grad_key = grad_qkv[:, query_cols : query_cols + kv_cols]
    grad_value = grad_qkv[:, query_cols + kv_cols :]
    grad_gain_one, grad_gain_two = gain_scatter(gain_one_part), gain_scatter(gain_two_part)
    return (
        output,
        input_grad,
        grad_gain_one,
        grad_query,
        grad_key,
        grad_value,
        grad_out,
        grad_gain_two,
        grad_gate,
        grad_up,
        grad_down,
    )


def solution(mesh):
    placed = (
        P(("wide", "tensor"), None),
        P("wide", None),
        P(("wide", "tensor")),
        P("wide", "tensor"),
        P("wide", "tensor"),
        P("wide", "tensor"),
        P("tensor", "wide"),
        P(("wide", "tensor")),
        P("wide", "tensor"),
        P("wide", "tensor"),
        P("tensor", "wide"),
        P(("wide", "tensor"), None),
    )
    return jax.shard_map(
        on_device,
        mesh=mesh,
        in_specs=placed,
        out_specs=(
            P(("wide", "tensor"), None),
            P(("wide", "tensor"), None),
            P(("wide", "tensor")),
            P("wide", "tensor"),
            P("wide", "tensor"),
            P("wide", "tensor"),
            P("tensor", "wide"),
            P(("wide", "tensor")),
            P("wide", "tensor"),
            P("wide", "tensor"),
            P("tensor", "wide"),
        ),
        check_vma=False,
    )
```

```python
import jax
import jax.numpy as jnp
from jax import lax
from jax.experimental import pallas as pl
from jax.experimental.pallas import tpu as pltpu
from jax.sharding import PartitionSpec as P

HEAD_DIM = 128
PROMPT = 1024


norm_eps = 1e-05
rope_base = 1000000.0
masked_score = -1e30


def swapped(block, axis, apart):
    count = lax.axis_size(axis)
    route = []
    for low in range(count):
        high = low | 1 << apart
        if high != low and high < count:
            route += [(low, high), (high, low)]
    return lax.ppermute(block, axis, route)


def layout(lengths_row, half_index, row_count, prompt_rows):
    cont_count = lengths_row.shape[0]
    ends_at = jnp.cumsum(lengths_row)
    starts_at = ends_at - lengths_row
    offsets = jnp.arange(row_count - prompt_rows, dtype=jnp.int32)
    which_cont = jnp.sum((offsets[:, None] >= ends_at[None, :]).astype(jnp.int32), axis=1)
    picked = (which_cont[:, None] == jnp.arange(cont_count, dtype=jnp.int32)[None, :]).astype(
        jnp.int32
    )
    begins = jnp.sum(picked * starts_at[None, :], axis=1)
    prompt_pos = half_index * prompt_rows + jnp.arange(prompt_rows, dtype=jnp.int32)
    cont_pos = 2 * prompt_rows + offsets - begins
    segment = jnp.concatenate([jnp.zeros((prompt_rows,), jnp.int32), which_cont + 1])
    position = jnp.concatenate([prompt_pos, cont_pos])
    return (segment, position)


def rope_tables(position, head_dim):
    half_dim = head_dim // 2
    inverse = rope_base ** (-jnp.arange(half_dim, dtype=jnp.float32) * (2.0 / head_dim))
    angles = position.astype(jnp.float32)[:, None] * inverse[None, :]
    cosine = jnp.cos(angles)
    sine_part = jnp.sin(angles)
    return (jnp.concatenate([cosine, cosine], 1), jnp.concatenate([sine_part, sine_part], 1))


def rotate(values, cosine, sine_part):
    half_dim = values.shape[-1] // 2
    turned = jnp.concatenate([-values[..., half_dim:], values[..., :half_dim]], -1)
    return values * cosine[:, None, :] + turned * sine_part[:, None, :]


def unrotate(grads, cosine, sine_part):
    half_dim = grads.shape[-1] // 2
    scaled = grads * sine_part[:, None, :]
    turned = jnp.concatenate([-scaled[..., half_dim:], scaled[..., :half_dim]], -1)
    return grads * cosine[:, None, :] - turned


def dot_rows(left, right):
    return lax.dot_general(
        left, right, (((0,), (0,)), ((), ())), preferred_element_type=jnp.float32
    )


def dot_back(left, right):
    return lax.dot_general(
        left, right, (((1,), (1,)), ((), ())), preferred_element_type=jnp.float32
    )


def meeting(bit, stride, count):
    return [(low, low ^ (bit * stride)) for low in range(count)]


class Square:
    def __init__(self, axis, stride):
        self.axis = axis
        self.stride = stride
        self.count = lax.axis_size(axis)
        self.place = lax.axis_index(axis) // stride % 4

    def meet(self, block, bit):
        return lax.ppermute(block, self.axis, meeting(bit, self.stride, self.count))

    def gather(self, own):
        first = self.meet(own, 1)
        second = self.meet(own, 2)
        cut = own.shape[0] // 2
        if cut == 0:
            return [own, first, second, self.meet(second, 1)]
        low_part = self.meet(second[:cut], 1)
        high_part = self.meet(first[cut:], 2)
        return [own, first, second, jnp.concatenate([low_part, high_part], 0)]

    def scatter(self, term_of):
        sent = jnp.bfloat16
        far = term_of(3).astype(sent)
        cut = far.shape[0] // 2
        low_part = self.meet(far[:cut], 1)
        high_part = self.meet(far[cut:], 2)
        first = term_of(1)
        second = term_of(2)
        first = jnp.concatenate([first[:cut], first[cut:] + high_part], 0).astype(sent)
        second = jnp.concatenate([second[:cut] + low_part, second[cut:]], 0).astype(sent)
        from_first = self.meet(first, 1)
        from_second = self.meet(second, 2)
        return term_of(0) + from_first.astype(jnp.float32) + from_second.astype(jnp.float32)

    def scatter_small(self, terms):
        def pick(j):
            return lax.dynamic_index_in_dim(terms, self.place ^ j, 0, keepdims=False)

        passed = pick(2) + self.meet(pick(3), 1)
        return pick(0) + self.meet(pick(1), 1) + self.meet(passed, 2)

    def ordered(self, slots, axis):
        extent = slots[0].shape[axis]
        shape = list(slots[0].shape)
        shape[axis] = 4 * extent
        whole = jnp.zeros(shape, slots[0].dtype)
        for j in range(4):
            whole = lax.dynamic_update_slice_in_dim(
                whole, slots[j], (self.place ^ j) * extent, axis
            )
        return whole


def twin(block):
    return lax.ppermute(block, "wide", meeting(1, 1, lax.axis_size("wide")))


def custom_mesh():
    return lax.axis_size("wide") == 8 and lax.axis_size("tensor") == 4


def wide_gather(own, axis):
    if not custom_mesh():
        return lax.all_gather(own, "wide", axis=axis, tiled=True)
    square = Square("wide", 2)
    core = lax.axis_index("wide") % 2
    slots = square.gather(own)
    extent = own.shape[axis]
    shape = list(own.shape)
    shape[axis] = 8 * extent
    whole = jnp.zeros(shape, own.dtype)
    for j in range(4):
        pair = (square.place ^ j) * 2
        whole = lax.dynamic_update_slice_in_dim(whole, slots[j], (pair + core) * extent, axis)
        whole = lax.dynamic_update_slice_in_dim(
            whole, twin(slots[j]), (pair + 1 - core) * extent, axis
        )
    return whole


def wide_scatter(grad, axis):
    if not custom_mesh():
        return lax.psum_scatter(
            grad.astype(jnp.bfloat16), "wide", scatter_dimension=axis, tiled=True
        ).astype(jnp.float32)
    square = Square("wide", 2)
    core = lax.axis_index("wide") % 2
    extent = grad.shape[axis] // 8
    grad_low = grad.astype(jnp.bfloat16)

    def term_of(j):
        pair = (square.place ^ j) * 2
        other = lax.dynamic_slice_in_dim(grad_low, (pair + 1 - core) * extent, extent, axis)
        mine = lax.dynamic_slice_in_dim(grad_low, (pair + core) * extent, extent, axis)
        return mine.astype(jnp.float32) + twin(other).astype(jnp.float32)

    return square.scatter(term_of)


def rows_gather(values):
    if not custom_mesh():
        return lax.all_gather(values, "tensor", axis=0, tiled=True)
    square = Square("tensor", 1)
    return jnp.concatenate(square.gather(values), 0)


def relative_rows(values, local_rows):
    if not custom_mesh():
        return values
    place = lax.axis_index("tensor")
    return jnp.concatenate(
        [lax.dynamic_slice_in_dim(values, (place ^ j) * local_rows, local_rows, 0) for j in range(4)],
        0,
    )


def prompt_start(prompt_rows):
    if not custom_mesh():
        return jnp.int32(0)
    return lax.axis_index("tensor") // 2 * prompt_rows


def rows_scatter(term_fn, local_rows):
    if not custom_mesh():
        return lax.psum_scatter(
            term_fn(0, local_rows * lax.axis_size("tensor")).astype(jnp.bfloat16),
            "tensor",
            scatter_dimension=0,
            tiled=True,
        ).astype(jnp.float32)
    square = Square("tensor", 1)
    far = term_fn(3 * local_rows, local_rows)
    near = term_fn(0, 3 * local_rows)
    terms = [near[j * local_rows : (j + 1) * local_rows] for j in range(3)] + [far]
    return square.scatter(lambda j: terms[j])


def gains_gather(gains):
    if not custom_mesh():
        return lax.all_gather(gains, ("wide", "tensor"), axis=1, tiled=True)
    own = gains[None]
    tensor_square = Square("tensor", 1)
    chip_square = Square("wide", 2)
    core = lax.axis_index("wide") % 2
    lanes = tensor_square.ordered(tensor_square.gather(own), 0)[None, None]
    other = twin(lanes)
    pair = jnp.where(
        core == 0, jnp.concatenate([lanes, other], 1), jnp.concatenate([other, lanes], 1)
    )
    whole = chip_square.ordered(chip_square.gather(pair), 0)
    return jnp.moveaxis(whole, 3, 0).reshape(gains.shape[0], -1)


def gain_scatter(part):
    if not custom_mesh():
        return lax.psum_scatter(part, ("wide", "tensor"), scatter_dimension=0, tiled=True)
    core = lax.axis_index("wide") % 2
    terms = part.reshape(4, 2, 4, -1)
    mine = lax.dynamic_index_in_dim(terms, core, 1, keepdims=False)
    other = lax.dynamic_index_in_dim(terms, 1 - core, 1, keepdims=False)
    chip_terms = Square("wide", 2).scatter_small(mine + twin(other))
    return Square("tensor", 1).scatter_small(chip_terms)


def rows_of(values, first_row, num_rows):
    return values[first_row : first_row + num_rows]


def column_scores(q_ref, k_ref, q_seg, q_pos, k_seg, k_pos, scale):
    scores = dot_back(k_ref[...], q_ref[...]) * scale
    allowed = ((k_seg[...] == 0) | (k_seg[...] == q_seg[...])) & (k_pos[...] <= q_pos[...])
    scores = jnp.where(allowed, scores, masked_score)
    exps = jnp.exp(scores - jnp.max(scores, axis=0, keepdims=True))
    return exps * (1.0 / jnp.sum(exps, axis=0, keepdims=True))


def attend_kernel(q_ref, k_ref, vt_ref, q_seg, q_pos, k_seg, k_pos, o_ref, *, scale):
    probs = column_scores(q_ref, k_ref, q_seg, q_pos, k_seg, k_pos, scale).astype(jnp.bfloat16)
    columns = jnp.dot(vt_ref[...], probs, preferred_element_type=jnp.float32)
    o_ref[...] = columns.T.astype(jnp.bfloat16)


def attend_back_kernel(
    q_ref, k_ref, kt_ref, v_ref, d_ref, cos_ref, sin_ref, q_seg, q_pos, k_seg, k_pos,
    dq_ref, dk_ref, dv_ref, *, scale,
):
    probs = column_scores(q_ref, k_ref, q_seg, q_pos, k_seg, k_pos, scale)
    d_probs = dot_back(v_ref[...], d_ref[...])
    term = jnp.sum(probs * d_probs, axis=0, keepdims=True)
    d_scores = (probs * (d_probs - term) * scale).astype(jnp.bfloat16)
    d_query = jnp.dot(kt_ref[...], d_scores, preferred_element_type=jnp.float32).T
    half_dim = d_query.shape[1] // 2
    lane = lax.broadcasted_iota(jnp.int32, d_query.shape, 1)
    turned = pltpu.roll(d_query, half_dim, 1)
    turned = jnp.where(lane < half_dim, -turned, turned)
    dq_ref[...] = (d_query * cos_ref[...] - turned * sin_ref[...]).astype(jnp.bfloat16)
    dk_part = jnp.dot(d_scores, q_ref[...], preferred_element_type=jnp.float32)
    dv_part = jnp.dot(
        probs.astype(jnp.bfloat16), d_ref[...], preferred_element_type=jnp.float32
    )
    first = (pl.program_id(1) == 0) & (pl.program_id(2) == 0)

    @pl.when(first)
    def _():
        dk_ref[...] = dk_part
        dv_ref[...] = dv_part

    @pl.when(jnp.logical_not(first))
    def _():
        dk_ref[...] += dk_part
        dv_ref[...] += dv_part


def attend_specs(block_rows, key_count, group_size, head_dim):
    def of_query(g, h, b):
        return (b, g * group_size + h)

    return dict(
        query=pl.BlockSpec((block_rows, head_dim), of_query),
        key=pl.BlockSpec((key_count, head_dim), lambda g, h, b: (0, g)),
        turned=pl.BlockSpec((head_dim, key_count), lambda g, h, b: (g, 0)),
        table=pl.BlockSpec((block_rows, head_dim), lambda g, h, b: (b, 0)),
        q_meta=pl.BlockSpec((1, block_rows), lambda g, h, b: (0, b)),
        k_meta=pl.BlockSpec((key_count, 1), lambda g, h, b: (0, 0)),
    )


def attend_forward(query, key, value, metas, head_dim, block_rows, scale):
    row_count, key_count = query.shape[0], key.shape[0]
    kv_heads = key.shape[1] // head_dim
    group_size = query.shape[1] // head_dim // kv_heads
    sp = attend_specs(block_rows, key_count, group_size, head_dim)

    def kernel(*refs):
        attend_kernel(*refs, scale=scale)

    return pl.pallas_call(
        kernel,
        grid=(kv_heads, group_size, row_count // block_rows),
        in_specs=[sp["query"], sp["key"], sp["turned"]] + [sp["q_meta"]] * 2 + [sp["k_meta"]] * 2,
        out_specs=sp["query"],
        out_shape=jax.ShapeDtypeStruct(query.shape, jnp.bfloat16),
    )(query, key, value.T, *metas)


def attend_backward(query, key, value, d_out, tables, metas, head_dim, block_rows, scale):
    row_count, key_count = query.shape[0], key.shape[0]
    kv_heads = key.shape[1] // head_dim
    group_size = query.shape[1] // head_dim // kv_heads
    sp = attend_specs(block_rows, key_count, group_size, head_dim)

    def kernel(*refs):
        attend_back_kernel(*refs, scale=scale)

    return pl.pallas_call(
        kernel,
        grid=(kv_heads, group_size, row_count // block_rows),
        in_specs=[sp["query"], sp["key"], sp["turned"], sp["key"], sp["query"]]
        + [sp["table"]] * 2
        + [sp["q_meta"]] * 2
        + [sp["k_meta"]] * 2,
        out_specs=[sp["query"], sp["key"], sp["key"]],
        out_shape=[
            jax.ShapeDtypeStruct(query.shape, jnp.bfloat16),
            jax.ShapeDtypeStruct(key.shape, jnp.float32),
            jax.ShapeDtypeStruct(key.shape, jnp.float32),
        ],
    )(query, key, key.T, value, d_out, *tables, *metas)


def on_device(
    layer_input,
    lengths,
    gain_attn,
    w_query,
    w_key,
    w_value,
    w_out,
    gain_ffn,
    w_gate,
    w_up,
    w_down,
    cotangent,
):
    tensor_count = lax.axis_size("tensor")
    local_rows = layer_input.shape[0]
    row_count = local_rows * tensor_count
    prompt_rows = PROMPT // 2
    head_dim = HEAD_DIM
    query_heads = w_query.shape[1] // head_dim
    kv_heads = w_key.shape[1] // head_dim
    group_size = query_heads // kv_heads
    score_scale = head_dim ** (-0.5)
    block_rows = min(256, row_count)
    half_index = lax.axis_index("wide") % 2
    low_type = jnp.bfloat16
    query_cols, kv_cols = w_query.shape[1], w_key.shape[1]
    hidden_cols = w_gate.shape[1]
    gains = gains_gather(jnp.stack([gain_attn, gain_ffn]))
    gain_one, gain_two = gains[0], gains[1]
    x_low_all = rows_gather(layer_input)
    qkv_wide = wide_gather(
        jnp.concatenate(
            [w_query.astype(low_type), w_key.astype(low_type), w_value.astype(low_type)], 1
        ),
        0,
    )
    o_wide = wide_gather(w_out.astype(low_type), 1)
    gate_up_wide = wide_gather(
        jnp.concatenate([w_gate.astype(low_type), w_up.astype(low_type)], 1), 0
    )
    down_wide = wide_gather(w_down.astype(low_type), 1)
    x_float = layer_input.astype(jnp.float32)
    inv_one = lax.rsqrt(jnp.mean(x_float * x_float, axis=-1, keepdims=True) + norm_eps)
    normed_one = x_float * inv_one
    x_all = x_low_all.astype(jnp.float32)
    normed_all = x_all * lax.rsqrt(jnp.mean(x_all * x_all, axis=-1, keepdims=True) + norm_eps)
    h_one_all = (normed_all * gain_one).astype(jnp.bfloat16)
    qkv_raw = jnp.dot(h_one_all, qkv_wide, preferred_element_type=jnp.float32)
    query_raw = qkv_raw[:, :query_cols]
    key_raw = qkv_raw[:, query_cols : query_cols + kv_cols]
    value_raw = qkv_raw[:, query_cols + kv_cols :]
    segment, position = layout(lengths[0], half_index, row_count, prompt_rows)
    segment = relative_rows(segment, local_rows)
    position = relative_rows(position, local_rows)
    prompt_at = prompt_start(prompt_rows)
    cosine, sine_part = rope_tables(position, head_dim)
    query_rot = rotate(
        query_raw.reshape(row_count, query_heads, head_dim), cosine, sine_part
    ).astype(jnp.bfloat16).reshape(row_count, query_heads * head_dim)
    key_rot = rotate(key_raw.reshape(row_count, kv_heads, head_dim), cosine, sine_part).astype(
        jnp.bfloat16
    ).reshape(row_count, kv_heads * head_dim)
    value_low = value_raw.astype(jnp.bfloat16)
    far_key, far_value = swapped(
        (
            lax.dynamic_slice_in_dim(key_rot, prompt_at, prompt_rows, 0),
            lax.dynamic_slice_in_dim(value_low, prompt_at, prompt_rows, 0),
        ),
        "wide",
        0,
    )
    key_all = jnp.concatenate([far_key, key_rot], 0)
    value_all = jnp.concatenate([far_value, value_low], 0)
    own_prompt = lax.dynamic_slice_in_dim(position, prompt_at, prompt_rows, 0)
    far_position = own_prompt + (1 - 2 * half_index) * prompt_rows
    key_segment = jnp.concatenate([jnp.zeros((prompt_rows,), jnp.int32), segment])
    key_position = jnp.concatenate([far_position, position])
    metas = (segment[None], position[None], key_segment[:, None], key_position[:, None])
    attn_low = attend_forward(
        query_rot, key_all, value_all, metas, head_dim, block_rows, score_scale
    )

    def attn_term(first_row, num_rows):
        return jnp.dot(rows_of(attn_low, first_row, num_rows), o_wide, preferred_element_type=jnp.float32)

    x_mid = x_float + rows_scatter(attn_term, local_rows)
    inv_two = lax.rsqrt(jnp.mean(x_mid * x_mid, axis=-1, keepdims=True) + norm_eps)
    normed_two = x_mid * inv_two
    h_two = (normed_two * gain_two).astype(jnp.bfloat16)
    h_two_all = rows_gather(h_two)
    gate_up_val = jnp.dot(h_two_all, gate_up_wide, preferred_element_type=jnp.float32)
    gate_val = gate_up_val[:, :hidden_cols]
    up_val = gate_up_val[:, hidden_cols:]
    gate_sig = jax.nn.sigmoid(gate_val)
    hidden_low = (gate_val * gate_sig * up_val).astype(jnp.bfloat16)

    def ffn_term(first_row, num_rows):
        return jnp.dot(rows_of(hidden_low, first_row, num_rows), down_wide, preferred_element_type=jnp.float32)

    output = (x_mid + rows_scatter(ffn_term, local_rows)).astype(jnp.bfloat16)
    cot_float = cotangent.astype(jnp.float32)
    cot_all = rows_gather(cotangent)
    d_hidden = dot_back(cot_all, down_wide)
    grad_down = dot_rows(hidden_low, cot_all)
    d_up = (d_hidden * gate_val * gate_sig).astype(jnp.bfloat16)
    d_gate = (d_hidden * up_val * gate_sig * (1.0 + gate_val * (1.0 - gate_sig))).astype(
        jnp.bfloat16
    )
    d_gate_up = jnp.concatenate([d_gate, d_up], 1)

    def ffn_back_term(first_row, num_rows):
        return dot_back(rows_of(d_gate_up, first_row, num_rows), gate_up_wide)

    d_h_two = rows_scatter(ffn_back_term, local_rows)
    grad_gate_up = dot_rows(h_two_all, d_gate_up)
    gain_two_part = jnp.sum(d_h_two * normed_two, axis=0)
    e_two = d_h_two * gain_two
    d_mid = cot_float + inv_two * (
        e_two - normed_two * jnp.mean(e_two * normed_two, axis=-1, keepdims=True)
    )
    d_mid_all = rows_gather(d_mid.astype(jnp.bfloat16))
    grad_out = dot_rows(attn_low, d_mid_all)
    d_attended = dot_back(d_mid_all, o_wide).astype(jnp.bfloat16)
    d_query_low, key_grad, value_grad = attend_backward(
        query_rot,
        key_all,
        value_all,
        d_attended,
        (cosine, sine_part),
        metas,
        head_dim,
        block_rows,
        score_scale,
    )
    far_key_grad, far_value_grad = (
        swapped(key_grad[:prompt_rows].astype(jnp.bfloat16), "wide", 0).astype(jnp.float32),
        swapped(value_grad[:prompt_rows].astype(jnp.bfloat16), "wide", 0).astype(jnp.float32),
    )

    def with_far(grads, far):
        own = grads[prompt_rows:]
        prompt_part = lax.dynamic_slice_in_dim(own, prompt_at, prompt_rows, 0) + far
        return lax.dynamic_update_slice_in_dim(own, prompt_part, prompt_at, 0)

    own_key_grad = with_far(key_grad, far_key_grad).reshape(row_count, kv_heads, head_dim)
    own_value_grad = with_far(value_grad, far_value_grad)
    d_key_low = (
        unrotate(own_key_grad, cosine, sine_part)
        .reshape(row_count, kv_heads * head_dim)
        .astype(jnp.bfloat16)
    )
    d_value_low = own_value_grad.astype(jnp.bfloat16)
    d_qkv_low = jnp.concatenate([d_query_low, d_key_low, d_value_low], 1)
    grad_qkv = dot_rows(h_one_all, d_qkv_low)

    def attn_back_term(first_row, num_rows):
        return dot_back(rows_of(d_qkv_low, first_row, num_rows), qkv_wide)

    d_h_one = rows_scatter(attn_back_term, local_rows)
    gain_one_part = jnp.sum(d_h_one * normed_one, axis=0)
    e_one = d_h_one * gain_one
    input_grad = (
        d_mid
        + inv_one * (e_one - normed_one * jnp.mean(e_one * normed_one, axis=-1, keepdims=True))
    ).astype(jnp.bfloat16)
    grad_down = wide_scatter(grad_down, 1)
    grad_gate_up = wide_scatter(grad_gate_up, 0)
    grad_out = wide_scatter(grad_out, 1)
    grad_qkv = wide_scatter(grad_qkv, 0)
    grad_gate, grad_up = grad_gate_up[:, :hidden_cols], grad_gate_up[:, hidden_cols:]
    grad_query = grad_qkv[:, :query_cols]
    grad_key = grad_qkv[:, query_cols : query_cols + kv_cols]
    grad_value = grad_qkv[:, query_cols + kv_cols :]
    grad_gain_one, grad_gain_two = gain_scatter(gain_one_part), gain_scatter(gain_two_part)
    return (
        output,
        input_grad,
        grad_gain_one,
        grad_query,
        grad_key,
        grad_value,
        grad_out,
        grad_gain_two,
        grad_gate,
        grad_up,
        grad_down,
    )


def solution(mesh):
    placed = (
        P(("wide", "tensor"), None),
        P("wide", None),
        P(("wide", "tensor")),
        P("wide", "tensor"),
        P("wide", "tensor"),
        P("wide", "tensor"),
        P("tensor", "wide"),
        P(("wide", "tensor")),
        P("wide", "tensor"),
        P("wide", "tensor"),
        P("tensor", "wide"),
        P(("wide", "tensor"), None),
    )
    return jax.shard_map(
        on_device,
        mesh=mesh,
        in_specs=placed,
        out_specs=(
            P(("wide", "tensor"), None),
            P(("wide", "tensor"), None),
            P(("wide", "tensor")),
            P("wide", "tensor"),
            P("wide", "tensor"),
            P("wide", "tensor"),
            P("tensor", "wide"),
            P(("wide", "tensor")),
            P("wide", "tensor"),
            P("wide", "tensor"),
            P("tensor", "wide"),
        ),
        check_vma=False,
    )
```

```python
import jax
import jax.numpy as jnp
from jax import lax
from jax.experimental import pallas as pl
from jax.experimental.pallas import tpu as pltpu
from jax.sharding import PartitionSpec as P

HEAD_DIM = 128
PROMPT = 1024


norm_eps = 1e-05
rope_base = 1000000.0
masked_score = -1e30


def swapped(block, axis, apart):
    count = lax.axis_size(axis)
    route = []
    for low in range(count):
        high = low | 1 << apart
        if high != low and high < count:
            route += [(low, high), (high, low)]
    return lax.ppermute(block, axis, route)


def layout(lengths_row, half_index, row_count, prompt_rows):
    cont_count = lengths_row.shape[0]
    ends_at = jnp.cumsum(lengths_row)
    starts_at = ends_at - lengths_row
    offsets = jnp.arange(row_count - prompt_rows, dtype=jnp.int32)
    which_cont = jnp.sum((offsets[:, None] >= ends_at[None, :]).astype(jnp.int32), axis=1)
    picked = (which_cont[:, None] == jnp.arange(cont_count, dtype=jnp.int32)[None, :]).astype(
        jnp.int32
    )
    begins = jnp.sum(picked * starts_at[None, :], axis=1)
    prompt_pos = half_index * prompt_rows + jnp.arange(prompt_rows, dtype=jnp.int32)
    cont_pos = 2 * prompt_rows + offsets - begins
    segment = jnp.concatenate([jnp.zeros((prompt_rows,), jnp.int32), which_cont + 1])
    position = jnp.concatenate([prompt_pos, cont_pos])
    return (segment, position)


def rope_tables(position, head_dim):
    half_dim = head_dim // 2
    inverse = rope_base ** (-jnp.arange(half_dim, dtype=jnp.float32) * (2.0 / head_dim))
    angles = position.astype(jnp.float32)[:, None] * inverse[None, :]
    cosine = jnp.cos(angles)
    sine_part = jnp.sin(angles)
    return (jnp.concatenate([cosine, cosine], 1), jnp.concatenate([sine_part, sine_part], 1))


def dot_rows(left, right):
    return lax.dot_general(
        left, right, (((0,), (0,)), ((), ())), preferred_element_type=jnp.float32
    )


def dot_back(left, right):
    return lax.dot_general(
        left, right, (((1,), (1,)), ((), ())), preferred_element_type=jnp.float32
    )


def meeting(bit, stride, count):
    return [(low, low ^ (bit * stride)) for low in range(count)]


class Square:
    def __init__(self, axis, stride):
        self.axis = axis
        self.stride = stride
        self.count = lax.axis_size(axis)
        self.place = lax.axis_index(axis) // stride % 4

    def meet(self, block, bit):
        return lax.ppermute(block, self.axis, meeting(bit, self.stride, self.count))

    def gather(self, own):
        first = self.meet(own, 1)
        second = self.meet(own, 2)
        cut = own.shape[0] // 2
        if cut == 0:
            return [own, first, second, self.meet(second, 1)]
        low_part = self.meet(second[:cut], 1)
        high_part = self.meet(first[cut:], 2)
        return [own, first, second, jnp.concatenate([low_part, high_part], 0)]

    def scatter(self, term_of):
        sent = jnp.bfloat16
        far = term_of(3).astype(sent)
        cut = far.shape[0] // 2
        low_part = self.meet(far[:cut], 1)
        high_part = self.meet(far[cut:], 2)
        first = term_of(1)
        second = term_of(2)
        first = jnp.concatenate([first[:cut], first[cut:] + high_part], 0).astype(sent)
        second = jnp.concatenate([second[:cut] + low_part, second[cut:]], 0).astype(sent)
        from_first = self.meet(first, 1)
        from_second = self.meet(second, 2)
        return term_of(0) + from_first.astype(jnp.float32) + from_second.astype(jnp.float32)

    def scatter_small(self, terms):
        def pick(j):
            return lax.dynamic_index_in_dim(terms, self.place ^ j, 0, keepdims=False)

        passed = pick(2) + self.meet(pick(3), 1)
        return pick(0) + self.meet(pick(1), 1) + self.meet(passed, 2)

    def ordered(self, slots, axis):
        extent = slots[0].shape[axis]
        shape = list(slots[0].shape)
        shape[axis] = 4 * extent
        whole = jnp.zeros(shape, slots[0].dtype)
        for j in range(4):
            whole = lax.dynamic_update_slice_in_dim(
                whole, slots[j], (self.place ^ j) * extent, axis
            )
        return whole


def twin(block):
    return lax.ppermute(block, "wide", meeting(1, 1, lax.axis_size("wide")))


def custom_mesh():
    return lax.axis_size("wide") == 8 and lax.axis_size("tensor") == 4


def after(values, earlier):
    return lax.optimization_barrier((values, earlier))[0]


def relative_columns(values):
    if not custom_mesh():
        return values
    extent = values.shape[-1] // 8
    place = lax.axis_index("wide")
    blocks = [
        lax.dynamic_slice_in_dim(values, (place ^ m) * extent, extent, values.ndim - 1)
        for m in range(8)
    ]
    return jnp.concatenate(blocks, -1)


def wide_gather(own):
    if not custom_mesh():
        whole = lax.all_gather(own, "wide", axis=0, tiled=True)
        return whole, whole
    slots = Square("wide", 2).gather(own)
    pairs = []
    for slot in slots:
        pairs += [slot, twin(slot)]
    return jnp.concatenate(pairs, 0), slots[3]


def wide_scatter(grad):
    if not custom_mesh():
        return lax.psum_scatter(
            grad.astype(jnp.bfloat16), "wide", scatter_dimension=0, tiled=True
        ).astype(jnp.float32)
    terms = grad.astype(jnp.bfloat16).reshape(4, 2, grad.shape[0] // 8, -1)
    arrived = twin(terms[:, 1])

    def term_of(j):
        return terms[j, 0].astype(jnp.float32) + arrived[j].astype(jnp.float32)

    return Square("wide", 2).scatter(term_of)


def rows_gather(values):
    if not custom_mesh():
        return lax.all_gather(values, "tensor", axis=0, tiled=True)
    square = Square("tensor", 1)
    return jnp.concatenate(square.gather(values), 0)


def relative_rows(values, local_rows):
    if not custom_mesh():
        return values
    place = lax.axis_index("tensor")
    return jnp.concatenate(
        [lax.dynamic_slice_in_dim(values, (place ^ j) * local_rows, local_rows, 0) for j in range(4)],
        0,
    )


def prompt_start(prompt_rows):
    if not custom_mesh():
        return jnp.int32(0)
    return lax.axis_index("tensor") // 2 * prompt_rows


def rows_scatter(term_fn, local_rows):
    if not custom_mesh():
        return lax.psum_scatter(
            term_fn(0, local_rows * lax.axis_size("tensor")).astype(jnp.bfloat16),
            "tensor",
            scatter_dimension=0,
            tiled=True,
        ).astype(jnp.float32)
    square = Square("tensor", 1)
    far = term_fn(3 * local_rows, local_rows)
    near = term_fn(0, 3 * local_rows)
    terms = [near[j * local_rows : (j + 1) * local_rows] for j in range(3)] + [far]
    return square.scatter(lambda j: terms[j])


def gains_gather(gains):
    if not custom_mesh():
        whole = lax.all_gather(gains, ("wide", "tensor"), axis=1, tiled=True)
        return whole, whole
    square = Square("tensor", 1)
    lanes = square.ordered(square.gather(gains[None]), 0)
    pair = jnp.stack([lanes, twin(lanes)])[None]
    whole = jnp.concatenate(Square("wide", 2).gather(pair), 0)
    return jnp.moveaxis(whole, 3, 0).reshape(gains.shape[0], -1), lanes


def gain_scatter(part):
    if not custom_mesh():
        return lax.psum_scatter(part, ("wide", "tensor"), scatter_dimension=0, tiled=True)
    terms = part.reshape(4, 2, 4, -1)
    terms = terms[:, 0] + twin(terms[:, 1])
    passed = terms[2] + Square("wide", 2).meet(terms[3], 1)
    chips = Square("wide", 2)
    terms = terms[0] + chips.meet(terms[1], 1) + chips.meet(passed, 2)
    return Square("tensor", 1).scatter_small(terms)


def rows_of(values, first_row, num_rows):
    return values[first_row : first_row + num_rows]


def rope_kernel(v_ref, cos_ref, sin_ref, o_ref, *, turned_heads):
    values = v_ref[...]
    half_dim = values.shape[1] // 2
    lane = lax.broadcasted_iota(jnp.int32, values.shape, 1)
    turned = pltpu.roll(values, half_dim, 1)
    turned = jnp.where(lane < half_dim, -turned, turned)
    rotated = values * cos_ref[...] + turned * sin_ref[...]
    plain = pl.program_id(0) >= turned_heads
    o_ref[...] = jnp.where(plain, values, rotated).astype(jnp.bfloat16)


def rope(values, tables, turned_heads, head_dim):
    rows = values.shape[0]
    block = pl.BlockSpec((rows, head_dim), lambda h: (0, h))
    table = pl.BlockSpec((rows, head_dim), lambda h: (0, 0))

    def kernel(*refs):
        rope_kernel(*refs, turned_heads=turned_heads)

    return pl.pallas_call(
        kernel,
        grid=(values.shape[1] // head_dim,),
        in_specs=[block, table, table],
        out_specs=block,
        out_shape=jax.ShapeDtypeStruct(values.shape, jnp.bfloat16),
    )(values, *tables)


def column_scores(q_ref, k_ref, q_seg, q_pos, k_seg, k_pos, scale):
    scores = dot_back(k_ref[...], q_ref[...]) * scale
    allowed = ((k_seg[...] == 0) | (k_seg[...] == q_seg[...])) & (k_pos[...] <= q_pos[...])
    scores = jnp.where(allowed, scores, masked_score)
    exps = jnp.exp(scores - jnp.max(scores, axis=0, keepdims=True))
    return exps * (1.0 / jnp.sum(exps, axis=0, keepdims=True))


def attend_kernel(q_ref, k_ref, vt_ref, q_seg, q_pos, k_seg, k_pos, o_ref, *, scale):
    probs = column_scores(q_ref, k_ref, q_seg, q_pos, k_seg, k_pos, scale).astype(jnp.bfloat16)
    columns = jnp.dot(vt_ref[...], probs, preferred_element_type=jnp.float32)
    o_ref[...] = columns.T.astype(jnp.bfloat16)


def attend_back_kernel(
    q_ref, k_ref, kt_ref, v_ref, d_ref, cos_ref, sin_ref, q_seg, q_pos, k_seg, k_pos,
    dq_ref, dk_ref, dv_ref, *, scale,
):
    probs = column_scores(q_ref, k_ref, q_seg, q_pos, k_seg, k_pos, scale)
    d_probs = dot_back(v_ref[...], d_ref[...])
    term = jnp.sum(probs * d_probs, axis=0, keepdims=True)
    d_scores = (probs * (d_probs - term) * scale).astype(jnp.bfloat16)
    d_query = jnp.dot(kt_ref[...], d_scores, preferred_element_type=jnp.float32).T
    half_dim = d_query.shape[1] // 2
    lane = lax.broadcasted_iota(jnp.int32, d_query.shape, 1)
    turned = pltpu.roll(d_query, half_dim, 1)
    turned = jnp.where(lane < half_dim, -turned, turned)
    dq_ref[...] = (d_query * cos_ref[...] - turned * sin_ref[...]).astype(jnp.bfloat16)
    dk_part = jnp.dot(d_scores, q_ref[...], preferred_element_type=jnp.float32)
    dv_part = jnp.dot(
        probs.astype(jnp.bfloat16), d_ref[...], preferred_element_type=jnp.float32
    )
    first = (pl.program_id(1) == 0) & (pl.program_id(2) == 0)

    @pl.when(first)
    def _():
        dk_ref[...] = dk_part
        dv_ref[...] = dv_part

    @pl.when(jnp.logical_not(first))
    def _():
        dk_ref[...] += dk_part
        dv_ref[...] += dv_part


def attend_specs(block_rows, key_count, group_size, head_dim):
    def of_query(g, h, b):
        return (b, g * group_size + h)

    return dict(
        query=pl.BlockSpec((block_rows, head_dim), of_query),
        key=pl.BlockSpec((key_count, head_dim), lambda g, h, b: (0, g)),
        turned=pl.BlockSpec((head_dim, key_count), lambda g, h, b: (g, 0)),
        table=pl.BlockSpec((block_rows, head_dim), lambda g, h, b: (b, 0)),
        q_meta=pl.BlockSpec((1, block_rows), lambda g, h, b: (0, b)),
        k_meta=pl.BlockSpec((key_count, 1), lambda g, h, b: (0, 0)),
    )


def attend_forward(query, key, value, metas, head_dim, block_rows, scale):
    row_count, key_count = query.shape[0], key.shape[0]
    kv_heads = key.shape[1] // head_dim
    group_size = query.shape[1] // head_dim // kv_heads
    sp = attend_specs(block_rows, key_count, group_size, head_dim)

    def kernel(*refs):
        attend_kernel(*refs, scale=scale)

    return pl.pallas_call(
        kernel,
        grid=(kv_heads, group_size, row_count // block_rows),
        in_specs=[sp["query"], sp["key"], sp["turned"]] + [sp["q_meta"]] * 2 + [sp["k_meta"]] * 2,
        out_specs=sp["query"],
        out_shape=jax.ShapeDtypeStruct(query.shape, jnp.bfloat16),
    )(query, key, value.T, *metas)


def attend_backward(query, key, value, d_out, tables, metas, head_dim, block_rows, scale):
    row_count, key_count = query.shape[0], key.shape[0]
    kv_heads = key.shape[1] // head_dim
    group_size = query.shape[1] // head_dim // kv_heads
    sp = attend_specs(block_rows, key_count, group_size, head_dim)

    def kernel(*refs):
        attend_back_kernel(*refs, scale=scale)

    return pl.pallas_call(
        kernel,
        grid=(kv_heads, group_size, row_count // block_rows),
        in_specs=[sp["query"], sp["key"], sp["turned"], sp["key"], sp["query"]]
        + [sp["table"]] * 2
        + [sp["q_meta"]] * 2
        + [sp["k_meta"]] * 2,
        out_specs=[sp["query"], sp["key"], sp["key"]],
        out_shape=[
            jax.ShapeDtypeStruct(query.shape, jnp.bfloat16),
            jax.ShapeDtypeStruct(key.shape, jnp.float32),
            jax.ShapeDtypeStruct(key.shape, jnp.float32),
        ],
    )(query, key, key.T, value, d_out, *tables, *metas)


def on_device(
    layer_input,
    lengths,
    gain_attn,
    w_query,
    w_key,
    w_value,
    w_out,
    gain_ffn,
    w_gate,
    w_up,
    w_down,
    cotangent,
):
    tensor_count = lax.axis_size("tensor")
    local_rows = layer_input.shape[0]
    row_count = local_rows * tensor_count
    prompt_rows = PROMPT // 2
    head_dim = HEAD_DIM
    query_heads = w_query.shape[1] // head_dim
    kv_heads = w_key.shape[1] // head_dim
    group_size = query_heads // kv_heads
    score_scale = head_dim ** (-0.5)
    block_rows = min(256, row_count)
    half_index = lax.axis_index("wide") % 2
    low_type = jnp.bfloat16
    query_cols, kv_cols = w_query.shape[1], w_key.shape[1]
    hidden_cols = w_gate.shape[1]
    gains, gains_near = gains_gather(jnp.stack([gain_attn, gain_ffn]))
    gain_one, gain_two = gains[0], gains[1]
    layer_input = relative_columns(layer_input)
    cotangent = relative_columns(cotangent)
    x_low_all = rows_gather(after(layer_input, gains_near))
    attn_own = jnp.concatenate([w_query, w_key, w_value, w_out.T], 1).astype(low_type)
    ffn_own = jnp.concatenate([w_gate, w_up, w_down.T], 1).astype(low_type)
    attn_wide, attn_far = wide_gather(after(attn_own, gains))
    qkv_cols = query_cols + 2 * kv_cols
    qkv_wide, out_wide = attn_wide[:, :qkv_cols], attn_wide[:, qkv_cols:]
    ffn_wide, _ = wide_gather(after(ffn_own, attn_far))
    gate_up_wide, down_wide = ffn_wide[:, : 2 * hidden_cols], ffn_wide[:, 2 * hidden_cols :]
    cot_all = rows_gather(after(cotangent, x_low_all))
    x_float = layer_input.astype(jnp.float32)
    inv_one = lax.rsqrt(jnp.mean(x_float * x_float, axis=-1, keepdims=True) + norm_eps)
    normed_one = x_float * inv_one
    x_all = x_low_all.astype(jnp.float32)
    normed_all = x_all * lax.rsqrt(jnp.mean(x_all * x_all, axis=-1, keepdims=True) + norm_eps)
    h_one_all = (normed_all * gain_one).astype(jnp.bfloat16)
    qkv_raw = jnp.dot(h_one_all, qkv_wide, preferred_element_type=jnp.float32)
    segment, position = layout(lengths[0], half_index, row_count, prompt_rows)
    segment = relative_rows(segment, local_rows)
    position = relative_rows(position, local_rows)
    prompt_at = prompt_start(prompt_rows)
    cosine, sine_part = rope_tables(position, head_dim)
    tables = (cosine, sine_part)
    qkv_low = rope(qkv_raw, tables, query_heads + kv_heads, head_dim)
    query_rot, kv_low = qkv_low[:, :query_cols], qkv_low[:, query_cols:]
    far_kv = swapped(
        lax.dynamic_slice_in_dim(kv_low, prompt_at, prompt_rows, 0), "wide", 0
    )
    kv_all = jnp.concatenate([far_kv, kv_low], 0)
    key_all, value_all = kv_all[:, :kv_cols], kv_all[:, kv_cols:]
    own_prompt = lax.dynamic_slice_in_dim(position, prompt_at, prompt_rows, 0)
    far_position = own_prompt + (1 - 2 * half_index) * prompt_rows
    key_segment = jnp.concatenate([jnp.zeros((prompt_rows,), jnp.int32), segment])
    key_position = jnp.concatenate([far_position, position])
    metas = (segment[None], position[None], key_segment[:, None], key_position[:, None])
    attn_low = attend_forward(
        query_rot, key_all, value_all, metas, head_dim, block_rows, score_scale
    )

    def attn_term(first_row, num_rows):
        return dot_back(rows_of(attn_low, first_row, num_rows), out_wide)

    x_mid = x_float + rows_scatter(attn_term, local_rows)
    inv_two = lax.rsqrt(jnp.mean(x_mid * x_mid, axis=-1, keepdims=True) + norm_eps)
    normed_two = x_mid * inv_two
    h_two = (normed_two * gain_two).astype(jnp.bfloat16)
    h_two_all = rows_gather(h_two)
    gate_up_val = jnp.dot(h_two_all, gate_up_wide, preferred_element_type=jnp.float32)
    gate_val = gate_up_val[:, :hidden_cols]
    up_val = gate_up_val[:, hidden_cols:]
    gate_sig = jax.nn.sigmoid(gate_val)
    hidden_low = (gate_val * gate_sig * up_val).astype(jnp.bfloat16)

    def ffn_term(first_row, num_rows):
        return dot_back(rows_of(hidden_low, first_row, num_rows), down_wide)

    output = (x_mid + rows_scatter(ffn_term, local_rows)).astype(jnp.bfloat16)
    cot_float = cotangent.astype(jnp.float32)
    d_hidden = jnp.dot(cot_all, down_wide, preferred_element_type=jnp.float32)
    grad_down = dot_rows(cot_all, hidden_low)
    d_up = (d_hidden * gate_val * gate_sig).astype(jnp.bfloat16)
    d_gate = (d_hidden * up_val * gate_sig * (1.0 + gate_val * (1.0 - gate_sig))).astype(
        jnp.bfloat16
    )
    d_gate_up = jnp.concatenate([d_gate, d_up], 1)

    def ffn_back_term(first_row, num_rows):
        return dot_back(rows_of(d_gate_up, first_row, num_rows), gate_up_wide)

    d_h_two = rows_scatter(ffn_back_term, local_rows)
    grad_gate_up = dot_rows(h_two_all, d_gate_up)
    gain_two_part = jnp.sum(d_h_two * normed_two, axis=0)
    e_two = d_h_two * gain_two
    d_mid = cot_float + inv_two * (
        e_two - normed_two * jnp.mean(e_two * normed_two, axis=-1, keepdims=True)
    )
    d_mid_all = rows_gather(d_mid.astype(jnp.bfloat16))
    grad_out = dot_rows(d_mid_all, attn_low)
    d_attended = jnp.dot(
        d_mid_all, out_wide, preferred_element_type=jnp.float32
    ).astype(jnp.bfloat16)
    d_query_low, key_grad, value_grad = attend_backward(
        query_rot,
        key_all,
        value_all,
        d_attended,
        tables,
        metas,
        head_dim,
        block_rows,
        score_scale,
    )
    kv_grad = jnp.concatenate([key_grad, value_grad], 1)
    far_grad = swapped(kv_grad[:prompt_rows].astype(low_type), "wide", 0)
    own_grad = kv_grad[prompt_rows:]
    prompt_part = lax.dynamic_slice_in_dim(own_grad, prompt_at, prompt_rows, 0)
    own_grad = lax.dynamic_update_slice_in_dim(
        own_grad, prompt_part + far_grad.astype(jnp.float32), prompt_at, 0
    )
    d_kv_low = rope(own_grad, (cosine, -sine_part), kv_heads, head_dim)
    d_qkv_low = jnp.concatenate([d_query_low, d_kv_low], 1)
    grad_qkv = dot_rows(h_one_all, d_qkv_low)

    def attn_back_term(first_row, num_rows):
        return dot_back(rows_of(d_qkv_low, first_row, num_rows), qkv_wide)

    d_h_one = rows_scatter(attn_back_term, local_rows)
    gain_one_part = jnp.sum(d_h_one * normed_one, axis=0)
    e_one = d_h_one * gain_one
    input_grad = (
        d_mid
        + inv_one * (e_one - normed_one * jnp.mean(e_one * normed_one, axis=-1, keepdims=True))
    ).astype(jnp.bfloat16)
    grad_down = wide_scatter(grad_down).T
    grad_gate_up = wide_scatter(grad_gate_up)
    grad_out = wide_scatter(grad_out).T
    grad_qkv = wide_scatter(grad_qkv)
    grad_gate, grad_up = grad_gate_up[:, :hidden_cols], grad_gate_up[:, hidden_cols:]
    grad_query = grad_qkv[:, :query_cols]
    grad_key = grad_qkv[:, query_cols : query_cols + kv_cols]
    grad_value = grad_qkv[:, query_cols + kv_cols :]
    grad_gain_one, grad_gain_two = gain_scatter(gain_one_part), gain_scatter(gain_two_part)
    return (
        relative_columns(output),
        relative_columns(input_grad),
        grad_gain_one,
        grad_query,
        grad_key,
        grad_value,
        grad_out,
        grad_gain_two,
        grad_gate,
        grad_up,
        grad_down,
    )


def solution(mesh):
    placed = (
        P(("wide", "tensor"), None),
        P("wide", None),
        P(("wide", "tensor")),
        P("wide", "tensor"),
        P("wide", "tensor"),
        P("wide", "tensor"),
        P("tensor", "wide"),
        P(("wide", "tensor")),
        P("wide", "tensor"),
        P("wide", "tensor"),
        P("tensor", "wide"),
        P(("wide", "tensor"), None),
    )
    return jax.shard_map(
        on_device,
        mesh=mesh,
        in_specs=placed,
        out_specs=(
            P(("wide", "tensor"), None),
            P(("wide", "tensor"), None),
            P(("wide", "tensor")),
            P("wide", "tensor"),
            P("wide", "tensor"),
            P("wide", "tensor"),
            P("tensor", "wide"),
            P(("wide", "tensor")),
            P("wide", "tensor"),
            P("wide", "tensor"),
            P("tensor", "wide"),
        ),
        check_vma=False,
    )
```

```python
import jax
import jax.numpy as jnp
from jax import lax
from jax.experimental import pallas as pl
from jax.experimental.pallas import tpu as pltpu
from jax.sharding import PartitionSpec as P

HEAD_DIM = 128
PROMPT = 1024


norm_eps = 1e-05
rope_base = 1000000.0
masked_score = -1e30


def swapped(block, axis, apart):
    count = lax.axis_size(axis)
    route = []
    for low in range(count):
        high = low | 1 << apart
        if high != low and high < count:
            route += [(low, high), (high, low)]
    return lax.ppermute(block, axis, route)


def layout(lengths_row, half_index, row_count, prompt_rows):
    cont_count = lengths_row.shape[0]
    ends_at = jnp.cumsum(lengths_row)
    starts_at = ends_at - lengths_row
    offsets = jnp.arange(row_count - prompt_rows, dtype=jnp.int32)
    which_cont = jnp.sum((offsets[:, None] >= ends_at[None, :]).astype(jnp.int32), axis=1)
    picked = (which_cont[:, None] == jnp.arange(cont_count, dtype=jnp.int32)[None, :]).astype(
        jnp.int32
    )
    begins = jnp.sum(picked * starts_at[None, :], axis=1)
    prompt_pos = half_index * prompt_rows + jnp.arange(prompt_rows, dtype=jnp.int32)
    cont_pos = 2 * prompt_rows + offsets - begins
    segment = jnp.concatenate([jnp.zeros((prompt_rows,), jnp.int32), which_cont + 1])
    position = jnp.concatenate([prompt_pos, cont_pos])
    return (segment, position)


def rope_tables(position, head_dim):
    half_dim = head_dim // 2
    inverse = rope_base ** (-jnp.arange(half_dim, dtype=jnp.float32) * (2.0 / head_dim))
    angles = position.astype(jnp.float32)[:, None] * inverse[None, :]
    cosine = jnp.cos(angles)
    sine_part = jnp.sin(angles)
    return (jnp.concatenate([cosine, cosine], 1), jnp.concatenate([sine_part, sine_part], 1))


def dot_rows(left, right):
    return lax.dot_general(
        left, right, (((0,), (0,)), ((), ())), preferred_element_type=jnp.float32
    )


def dot_back(left, right):
    return lax.dot_general(
        left, right, (((1,), (1,)), ((), ())), preferred_element_type=jnp.float32
    )


def meeting(bit, stride, count):
    return [(low, low ^ (bit * stride)) for low in range(count)]


class Square:
    def __init__(self, axis, stride):
        self.axis = axis
        self.stride = stride
        self.count = lax.axis_size(axis)
        self.place = lax.axis_index(axis) // stride % 4

    def meet(self, block, bit):
        return lax.ppermute(block, self.axis, meeting(bit, self.stride, self.count))

    def gather(self, own):
        first = self.meet(own, 1)
        second = self.meet(own, 2)
        cut = own.shape[0] // 2
        low_part = self.meet(second[:cut], 1)
        high_part = self.meet(first[cut:], 2)
        return [own, first, second, jnp.concatenate([low_part, high_part], 0)]

    def gather_small(self, own):
        return [own] + [self.meet(own, bits) for bits in (1, 2, 3)]

    def scatter(self, far, near_of):
        sent = jnp.bfloat16
        cut = far.shape[0] // 2
        low_part = self.meet(far[:cut], 1)
        high_part = self.meet(far[cut:], 2)
        own, first, second = near_of()
        first = jnp.concatenate([first[:cut], first[cut:] + high_part], 0).astype(sent)
        second = jnp.concatenate([second[:cut] + low_part, second[cut:]], 0).astype(sent)
        from_first = self.meet(first, 1)
        from_second = self.meet(second, 2)
        total = own + from_first.astype(jnp.float32) + from_second.astype(jnp.float32)
        return total, (first, second)

    def scatter_small(self, terms):
        def pick(j):
            return lax.dynamic_index_in_dim(terms, self.place ^ j, 0, keepdims=False)

        passed = pick(2) + self.meet(pick(3), 1)
        return pick(0) + self.meet(pick(1), 1) + self.meet(passed, 2)

    def ordered(self, slots, axis):
        extent = slots[0].shape[axis]
        shape = list(slots[0].shape)
        shape[axis] = 4 * extent
        whole = jnp.zeros(shape, slots[0].dtype)
        for j in range(4):
            whole = lax.dynamic_update_slice_in_dim(
                whole, slots[j], (self.place ^ j) * extent, axis
            )
        return whole


def twin(block):
    return lax.ppermute(block, "wide", meeting(1, 1, lax.axis_size("wide")))


def custom_mesh():
    return lax.axis_size("wide") == 8 and lax.axis_size("tensor") == 4


def after(values, earlier):
    return lax.optimization_barrier((values, earlier))[0]


def relative_columns(values):
    if not custom_mesh():
        return values
    extent = values.shape[-1] // 8
    place = lax.axis_index("wide")
    blocks = [
        lax.dynamic_slice_in_dim(values, (place ^ m) * extent, extent, values.ndim - 1)
        for m in range(8)
    ]
    return jnp.concatenate(blocks, -1)


def wide_gather(own):
    if not custom_mesh():
        whole = lax.all_gather(own, "wide", axis=0, tiled=True)
        return whole, whole
    slots = Square("wide", 2).gather(own)
    pairs = []
    for slot in slots:
        pairs += [slot, twin(slot)]
    return jnp.concatenate(pairs, 0), slots[3]


def wide_scatter(grad, earlier=None):
    grad = grad.astype(jnp.bfloat16)
    if not custom_mesh():
        total = lax.psum_scatter(grad, "wide", scatter_dimension=0, tiled=True).astype(jnp.float32)
        return total, total, total
    terms = grad.reshape(4, 2, grad.shape[0] // 8, -1)
    others = terms[:, 1]
    if earlier is not None:
        others = after(others, earlier)
    arrived = twin(others)

    def term_of(j):
        return terms[j, 0].astype(jnp.float32) + arrived[j].astype(jnp.float32)

    far = term_of(3).astype(jnp.bfloat16)
    total, passed_on = Square("wide", 2).scatter(far, lambda: [term_of(j) for j in range(3)])
    return total, far, passed_on


def rows_gather(values):
    if not custom_mesh():
        return lax.all_gather(values, "tensor", axis=0, tiled=True)
    square = Square("tensor", 1)
    return jnp.concatenate(square.gather(values), 0)


def relative_rows(values, local_rows):
    if not custom_mesh():
        return values
    place = lax.axis_index("tensor")
    return jnp.concatenate(
        [lax.dynamic_slice_in_dim(values, (place ^ j) * local_rows, local_rows, 0) for j in range(4)],
        0,
    )


def prompt_start(prompt_rows):
    if not custom_mesh():
        return jnp.int32(0)
    return lax.axis_index("tensor") // 2 * prompt_rows


def rows_scatter(term_fn, local_rows, earlier=None):
    if not custom_mesh():
        total = lax.psum_scatter(
            term_fn(0, local_rows * lax.axis_size("tensor"), None).astype(jnp.bfloat16),
            "tensor",
            scatter_dimension=0,
            tiled=True,
        ).astype(jnp.float32)
        return total, total
    far = term_fn(3 * local_rows, local_rows, None).astype(jnp.bfloat16)
    if earlier is not None:
        far = after(far, earlier)

    def near_of():
        near = term_fn(0, 3 * local_rows, far)
        return [near[j * local_rows : (j + 1) * local_rows] for j in range(3)]

    return Square("tensor", 1).scatter(far, near_of)


def gains_gather(gains):
    if not custom_mesh():
        whole = lax.all_gather(gains, ("wide", "tensor"), axis=1, tiled=True)
        return whole, whole
    square = Square("tensor", 1)
    lanes = square.ordered(square.gather_small(gains[None]), 0)
    pair = jnp.stack([lanes, twin(lanes)])[None]
    whole = jnp.concatenate(Square("wide", 2).gather_small(pair), 0)
    return jnp.moveaxis(whole, 3, 0).reshape(gains.shape[0], -1), lanes


def gain_scatter(part):
    if not custom_mesh():
        return lax.psum_scatter(part, ("wide", "tensor"), scatter_dimension=0, tiled=True)
    terms = part.reshape(4, 2, 4, -1)
    kept = part.shape[1]
    terms = terms[:, 0] + twin(terms[:, 1])
    passed = terms[2] + Square("wide", 2).meet(terms[3], 1)
    chips = Square("wide", 2)
    terms = terms[0] + chips.meet(terms[1], 1) + chips.meet(passed, 2)
    return Square("tensor", 1).scatter_small(terms).reshape(-1, kept)


def rows_of(values, first_row, num_rows, earlier):
    rows = values[first_row : first_row + num_rows]
    return rows if earlier is None else after(rows, earlier)


def rope_kernel(v_ref, cos_ref, sin_ref, o_ref, *, turned_heads):
    values = v_ref[...]
    half_dim = values.shape[1] // 2
    lane = lax.broadcasted_iota(jnp.int32, values.shape, 1)
    turned = pltpu.roll(values, half_dim, 1)
    turned = jnp.where(lane < half_dim, -turned, turned)
    rotated = values * cos_ref[...] + turned * sin_ref[...]
    plain = pl.program_id(0) >= turned_heads
    o_ref[...] = jnp.where(plain, values, rotated).astype(jnp.bfloat16)


def rope(values, tables, turned_heads, head_dim):
    rows = values.shape[0]
    block = pl.BlockSpec((rows, head_dim), lambda h: (0, h))
    table = pl.BlockSpec((rows, head_dim), lambda h: (0, 0))

    def kernel(*refs):
        rope_kernel(*refs, turned_heads=turned_heads)

    return pl.pallas_call(
        kernel,
        grid=(values.shape[1] // head_dim,),
        in_specs=[block, table, table],
        out_specs=block,
        out_shape=jax.ShapeDtypeStruct(values.shape, jnp.bfloat16),
    )(values, *tables)


def column_scores(q_ref, k_ref, q_seg, q_pos, k_seg, k_pos, scale):
    scores = dot_back(k_ref[...], q_ref[...]) * scale
    allowed = ((k_seg[...] == 0) | (k_seg[...] == q_seg[...])) & (k_pos[...] <= q_pos[...])
    scores = jnp.where(allowed, scores, masked_score)
    exps = jnp.exp(scores - jnp.max(scores, axis=0, keepdims=True))
    return exps * (1.0 / jnp.sum(exps, axis=0, keepdims=True))


def attend_kernel(q_ref, k_ref, vt_ref, q_seg, q_pos, k_seg, k_pos, o_ref, *, scale):
    probs = column_scores(q_ref, k_ref, q_seg, q_pos, k_seg, k_pos, scale).astype(jnp.bfloat16)
    columns = jnp.dot(vt_ref[...], probs, preferred_element_type=jnp.float32)
    o_ref[...] = columns.T.astype(jnp.bfloat16)


def attend_back_kernel(
    q_ref, k_ref, kt_ref, v_ref, d_ref, cos_ref, sin_ref, q_seg, q_pos, k_seg, k_pos,
    dq_ref, dk_ref, dv_ref, *, scale,
):
    probs = column_scores(q_ref, k_ref, q_seg, q_pos, k_seg, k_pos, scale)
    d_probs = dot_back(v_ref[...], d_ref[...])
    term = jnp.sum(probs * d_probs, axis=0, keepdims=True)
    d_scores = (probs * (d_probs - term) * scale).astype(jnp.bfloat16)
    d_query = jnp.dot(kt_ref[...], d_scores, preferred_element_type=jnp.float32).T
    half_dim = d_query.shape[1] // 2
    lane = lax.broadcasted_iota(jnp.int32, d_query.shape, 1)
    turned = pltpu.roll(d_query, half_dim, 1)
    turned = jnp.where(lane < half_dim, -turned, turned)
    dq_ref[...] = (d_query * cos_ref[...] - turned * sin_ref[...]).astype(jnp.bfloat16)
    dk_part = jnp.dot(d_scores, q_ref[...], preferred_element_type=jnp.float32)
    dv_part = jnp.dot(
        probs.astype(jnp.bfloat16), d_ref[...], preferred_element_type=jnp.float32
    )
    first = (pl.program_id(1) == 0) & (pl.program_id(2) == 0)

    @pl.when(first)
    def _():
        dk_ref[...] = dk_part
        dv_ref[...] = dv_part

    @pl.when(jnp.logical_not(first))
    def _():
        dk_ref[...] += dk_part
        dv_ref[...] += dv_part


def attend_specs(block_rows, key_count, group_size, head_dim):
    def of_query(g, h, b):
        return (b, g * group_size + h)

    return dict(
        query=pl.BlockSpec((block_rows, head_dim), of_query),
        key=pl.BlockSpec((key_count, head_dim), lambda g, h, b: (0, g)),
        turned=pl.BlockSpec((head_dim, key_count), lambda g, h, b: (g, 0)),
        table=pl.BlockSpec((block_rows, head_dim), lambda g, h, b: (b, 0)),
        q_meta=pl.BlockSpec((1, block_rows), lambda g, h, b: (0, b)),
        k_meta=pl.BlockSpec((key_count, 1), lambda g, h, b: (0, 0)),
    )


def attend_forward(query, key, value, metas, head_dim, block_rows, scale):
    row_count, key_count = query.shape[0], key.shape[0]
    kv_heads = key.shape[1] // head_dim
    group_size = query.shape[1] // head_dim // kv_heads
    sp = attend_specs(block_rows, key_count, group_size, head_dim)

    def kernel(*refs):
        attend_kernel(*refs, scale=scale)

    return pl.pallas_call(
        kernel,
        grid=(kv_heads, group_size, row_count // block_rows),
        in_specs=[sp["query"], sp["key"], sp["turned"]] + [sp["q_meta"]] * 2 + [sp["k_meta"]] * 2,
        out_specs=sp["query"],
        out_shape=jax.ShapeDtypeStruct(query.shape, jnp.bfloat16),
    )(query, key, value.T, *metas)


def attend_backward(query, key, value, d_out, tables, metas, head_dim, block_rows, scale):
    row_count, key_count = query.shape[0], key.shape[0]
    kv_heads = key.shape[1] // head_dim
    group_size = query.shape[1] // head_dim // kv_heads
    sp = attend_specs(block_rows, key_count, group_size, head_dim)

    def kernel(*refs):
        attend_back_kernel(*refs, scale=scale)

    return pl.pallas_call(
        kernel,
        grid=(kv_heads, group_size, row_count // block_rows),
        in_specs=[sp["query"], sp["key"], sp["turned"], sp["key"], sp["query"]]
        + [sp["table"]] * 2
        + [sp["q_meta"]] * 2
        + [sp["k_meta"]] * 2,
        out_specs=[sp["query"], sp["key"], sp["key"]],
        out_shape=[
            jax.ShapeDtypeStruct(query.shape, jnp.bfloat16),
            jax.ShapeDtypeStruct(key.shape, jnp.float32),
            jax.ShapeDtypeStruct(key.shape, jnp.float32),
        ],
    )(query, key, key.T, value, d_out, *tables, *metas)


def on_device(
    layer_input,
    lengths,
    gain_attn,
    w_query,
    w_key,
    w_value,
    w_out,
    gain_ffn,
    w_gate,
    w_up,
    w_down,
    cotangent,
):
    tensor_count = lax.axis_size("tensor")
    local_rows = layer_input.shape[0]
    row_count = local_rows * tensor_count
    prompt_rows = PROMPT // 2
    head_dim = HEAD_DIM
    query_heads = w_query.shape[1] // head_dim
    kv_heads = w_key.shape[1] // head_dim
    group_size = query_heads // kv_heads
    score_scale = head_dim ** (-0.5)
    block_rows = min(256, row_count)
    half_index = lax.axis_index("wide") % 2
    low_type = jnp.bfloat16
    query_cols, kv_cols = w_query.shape[1], w_key.shape[1]
    hidden_cols = w_gate.shape[1]
    gains, _ = gains_gather(jnp.stack([gain_attn, gain_ffn]))
    gain_one, gain_two = gains[0], gains[1]
    layer_input = relative_columns(layer_input)
    cotangent = relative_columns(cotangent)
    x_low_all = rows_gather(layer_input)
    attn_own = jnp.concatenate([w_query, w_key, w_value, w_out.T], 1).astype(low_type)
    ffn_own = jnp.concatenate([w_gate, w_up, w_down.T], 1).astype(low_type)
    attn_wide, attn_far = wide_gather(attn_own)
    qkv_cols = query_cols + 2 * kv_cols
    qkv_wide, out_wide = attn_wide[:, :qkv_cols], attn_wide[:, qkv_cols:]
    ffn_wide, _ = wide_gather(after(ffn_own, attn_far))
    gate_up_wide, down_wide = ffn_wide[:, : 2 * hidden_cols], ffn_wide[:, 2 * hidden_cols :]
    cot_all = rows_gather(after(cotangent, x_low_all))
    x_float = layer_input.astype(jnp.float32)
    inv_one = lax.rsqrt(jnp.mean(x_float * x_float, axis=-1, keepdims=True) + norm_eps)
    normed_one = x_float * inv_one
    x_all = x_low_all.astype(jnp.float32)
    normed_all = x_all * lax.rsqrt(jnp.mean(x_all * x_all, axis=-1, keepdims=True) + norm_eps)
    h_one_all = (normed_all * gain_one).astype(jnp.bfloat16)
    qkv_raw = jnp.dot(h_one_all, qkv_wide, preferred_element_type=jnp.float32)
    segment, position = layout(lengths[0], half_index, row_count, prompt_rows)
    segment = relative_rows(segment, local_rows)
    position = relative_rows(position, local_rows)
    prompt_at = prompt_start(prompt_rows)
    cosine, sine_part = rope_tables(position, head_dim)
    tables = (cosine, sine_part)
    qkv_low = rope(qkv_raw, tables, query_heads + kv_heads, head_dim)
    query_rot, kv_low = qkv_low[:, :query_cols], qkv_low[:, query_cols:]
    far_kv = swapped(
        lax.dynamic_slice_in_dim(kv_low, prompt_at, prompt_rows, 0), "wide", 0
    )
    kv_all = jnp.concatenate([far_kv, kv_low], 0)
    key_all, value_all = kv_all[:, :kv_cols], kv_all[:, kv_cols:]
    own_prompt = lax.dynamic_slice_in_dim(position, prompt_at, prompt_rows, 0)
    far_position = own_prompt + (1 - 2 * half_index) * prompt_rows
    key_segment = jnp.concatenate([jnp.zeros((prompt_rows,), jnp.int32), segment])
    key_position = jnp.concatenate([far_position, position])
    span = group_size * head_dim
    metas = (segment[None], position[None], key_segment[:, None], key_position[:, None])
    head_query = [query_rot[:, g * span : (g + 1) * span] for g in range(kv_heads)]
    head_key = [key_all[:, g * head_dim : (g + 1) * head_dim] for g in range(kv_heads)]
    head_value = [value_all[:, g * head_dim : (g + 1) * head_dim] for g in range(kv_heads)]
    attn_parts = []
    for g in range(kv_heads):
        attn_parts.append(
            attend_forward(
                head_query[g],
                head_key[g],
                head_value[g],
                metas,
                head_dim,
                block_rows,
                score_scale,
            )
        )
    attn_low = jnp.concatenate(attn_parts, 1)

    def attn_term(first_row, num_rows, earlier):
        return dot_back(rows_of(attn_low, first_row, num_rows, earlier), out_wide)

    attn_sum, _ = rows_scatter(attn_term, local_rows, cot_all)
    x_mid = x_float + attn_sum
    inv_two = lax.rsqrt(jnp.mean(x_mid * x_mid, axis=-1, keepdims=True) + norm_eps)
    normed_two = x_mid * inv_two
    h_two = (normed_two * gain_two).astype(jnp.bfloat16)
    h_two_all = rows_gather(h_two)
    gate_up_val = jnp.dot(h_two_all, gate_up_wide, preferred_element_type=jnp.float32)
    gate_val = gate_up_val[:, :hidden_cols]
    up_val = gate_up_val[:, hidden_cols:]
    gate_sig = jax.nn.sigmoid(gate_val)
    hidden_low = (gate_val * gate_sig * up_val).astype(jnp.bfloat16)

    cot_float = cotangent.astype(jnp.float32)
    d_hidden = jnp.dot(cot_all, down_wide, preferred_element_type=jnp.float32)
    d_up = (d_hidden * gate_val * gate_sig).astype(jnp.bfloat16)
    d_gate = (d_hidden * up_val * gate_sig * (1.0 + gate_val * (1.0 - gate_sig))).astype(
        jnp.bfloat16
    )
    d_gate_up = jnp.concatenate([d_gate, d_up], 1)

    def ffn_back_term(first_row, num_rows, earlier):
        return dot_back(rows_of(d_gate_up, first_row, num_rows, earlier), gate_up_wide)

    d_h_two, passed_on = rows_scatter(ffn_back_term, local_rows)
    d_gate_up_late, hidden_late = after((d_gate_up, hidden_low), passed_on)
    grad_gate_up = dot_rows(h_two_all, d_gate_up_late)
    grad_down = dot_rows(cot_all, hidden_late)
    gain_two_part = jnp.sum(d_h_two * normed_two, axis=0)
    e_two = d_h_two * gain_two
    d_mid = cot_float + inv_two * (
        e_two - normed_two * jnp.mean(e_two * normed_two, axis=-1, keepdims=True)
    )
    d_mid_all = rows_gather(d_mid.astype(jnp.bfloat16))

    def ffn_term(first_row, num_rows, earlier):
        return dot_back(rows_of(hidden_late, first_row, num_rows, earlier), down_wide)

    ffn_sum, _ = rows_scatter(ffn_term, local_rows, d_mid_all)
    output = (x_mid + ffn_sum).astype(jnp.bfloat16)
    grad_out = dot_rows(d_mid_all, attn_low)
    d_attended = jnp.dot(
        d_mid_all, out_wide, preferred_element_type=jnp.float32
    ).astype(jnp.bfloat16)
    grad_gate_up, _, gate_up_passed = wide_scatter(grad_gate_up)
    grad_down, _, down_passed = wide_scatter(grad_down)
    grad_out, _, _ = wide_scatter(grad_out, (gate_up_passed, down_passed))
    back = []
    for g in range(kv_heads):
        d_head = d_attended[:, g * span : (g + 1) * span]
        if g:
            d_head = after(d_head, back[g - 1][0])
        back.append(
            attend_backward(
                head_query[g],
                head_key[g],
                head_value[g],
                d_head,
                tables,
                metas,
                head_dim,
                block_rows,
                score_scale,
            )
        )
    d_query_low = jnp.concatenate([part[0] for part in back], 1)
    key_grad = jnp.concatenate([part[1] for part in back], 1)
    value_grad = jnp.concatenate([part[2] for part in back], 1)
    kv_grad = jnp.concatenate([key_grad, value_grad], 1)
    far_grad = swapped(kv_grad[:prompt_rows].astype(low_type), "wide", 0)
    own_grad = kv_grad[prompt_rows:]
    prompt_part = lax.dynamic_slice_in_dim(own_grad, prompt_at, prompt_rows, 0)
    own_grad = lax.dynamic_update_slice_in_dim(
        own_grad, prompt_part + far_grad.astype(jnp.float32), prompt_at, 0
    )
    d_kv_low = rope(own_grad, (cosine, -sine_part), kv_heads, head_dim)
    d_qkv_low = jnp.concatenate([d_query_low, d_kv_low], 1)

    def attn_back_term(first_row, num_rows, earlier):
        return dot_back(rows_of(d_qkv_low, first_row, num_rows, earlier), qkv_wide)

    d_h_one, passed_on = rows_scatter(attn_back_term, local_rows)
    grad_qkv = dot_rows(h_one_all, after(d_qkv_low, passed_on))
    gain_one_part = jnp.sum(d_h_one * normed_one, axis=0)
    e_one = d_h_one * gain_one
    input_grad = (
        d_mid
        + inv_one * (e_one - normed_one * jnp.mean(e_one * normed_one, axis=-1, keepdims=True))
    ).astype(jnp.bfloat16)
    grad_qkv, _, _ = wide_scatter(grad_qkv, (grad_gate_up, grad_down))
    grad_down, grad_out = grad_down.T, grad_out.T
    grad_gate, grad_up = grad_gate_up[:, :hidden_cols], grad_gate_up[:, hidden_cols:]
    grad_query = grad_qkv[:, :query_cols]
    grad_key = grad_qkv[:, query_cols : query_cols + kv_cols]
    grad_value = grad_qkv[:, query_cols + kv_cols :]
    gain_grads = gain_scatter(jnp.stack([gain_one_part, gain_two_part], 1))
    grad_gain_one, grad_gain_two = gain_grads[:, 0], gain_grads[:, 1]
    return (
        relative_columns(output),
        relative_columns(input_grad),
        grad_gain_one,
        grad_query,
        grad_key,
        grad_value,
        grad_out,
        grad_gain_two,
        grad_gate,
        grad_up,
        grad_down,
    )


def solution(mesh):
    placed = (
        P(("wide", "tensor"), None),
        P("wide", None),
        P(("wide", "tensor")),
        P("wide", "tensor"),
        P("wide", "tensor"),
        P("wide", "tensor"),
        P("tensor", "wide"),
        P(("wide", "tensor")),
        P("wide", "tensor"),
        P("wide", "tensor"),
        P("tensor", "wide"),
        P(("wide", "tensor"), None),
    )

    return jax.shard_map(
        on_device,
        mesh=mesh,
        in_specs=placed,
        out_specs=(
            P(("wide", "tensor"), None),
            P(("wide", "tensor"), None),
            P(("wide", "tensor")),
            P("wide", "tensor"),
            P("wide", "tensor"),
            P("wide", "tensor"),
            P("tensor", "wide"),
            P(("wide", "tensor")),
            P("wide", "tensor"),
            P("wide", "tensor"),
            P("tensor", "wide"),
        ),
        check_vma=False,
    )
```

```python
import jax
import jax.numpy as jnp
from jax import lax
from jax.experimental import pallas as pl
from jax.experimental.pallas import tpu as pltpu
from jax.sharding import PartitionSpec as P

HEAD_DIM = 128
PROMPT = 1024


norm_eps = 1e-05
rope_base = 1000000.0
masked_score = -1e30


def swapped(block, axis, apart):
    count = lax.axis_size(axis)
    route = []
    for low in range(count):
        high = low | 1 << apart
        if high != low and high < count:
            route += [(low, high), (high, low)]
    return lax.ppermute(block, axis, route)


def layout(lengths_row, half_index, row_count, prompt_rows):
    cont_count = lengths_row.shape[0]
    ends_at = jnp.cumsum(lengths_row)
    starts_at = ends_at - lengths_row
    offsets = jnp.arange(row_count - prompt_rows, dtype=jnp.int32)
    which_cont = jnp.sum((offsets[:, None] >= ends_at[None, :]).astype(jnp.int32), axis=1)
    picked = (which_cont[:, None] == jnp.arange(cont_count, dtype=jnp.int32)[None, :]).astype(
        jnp.int32
    )
    begins = jnp.sum(picked * starts_at[None, :], axis=1)
    prompt_pos = half_index * prompt_rows + jnp.arange(prompt_rows, dtype=jnp.int32)
    cont_pos = 2 * prompt_rows + offsets - begins
    segment = jnp.concatenate([jnp.zeros((prompt_rows,), jnp.int32), which_cont + 1])
    position = jnp.concatenate([prompt_pos, cont_pos])
    return (segment, position)


def rope_tables(position, head_dim):
    half_dim = head_dim // 2
    inverse = rope_base ** (-jnp.arange(half_dim, dtype=jnp.float32) * (2.0 / head_dim))
    angles = position.astype(jnp.float32)[:, None] * inverse[None, :]
    cosine = jnp.cos(angles)
    sine_part = jnp.sin(angles)
    return (jnp.concatenate([cosine, cosine], 1), jnp.concatenate([sine_part, sine_part], 1))


def dot_rows(left, right):
    return lax.dot_general(
        left, right, (((0,), (0,)), ((), ())), preferred_element_type=jnp.float32
    )


def dot_back(left, right):
    return lax.dot_general(
        left, right, (((1,), (1,)), ((), ())), preferred_element_type=jnp.float32
    )


def meeting(bit, stride, count):
    return [(low, low ^ (bit * stride)) for low in range(count)]


class Square:
    def __init__(self, axis, stride):
        self.axis = axis
        self.stride = stride
        self.count = lax.axis_size(axis)
        self.place = lax.axis_index(axis) // stride % 4

    def meet(self, block, bit):
        return lax.ppermute(block, self.axis, meeting(bit, self.stride, self.count))

    def gather(self, own):
        first = self.meet(own, 1)
        second = self.meet(own, 2)
        cut = own.shape[0] // 2
        low_part = self.meet(second[:cut], 1)
        high_part = self.meet(first[cut:], 2)
        return [own, first, second, jnp.concatenate([low_part, high_part], 0)]

    def gather_small(self, own):
        return [own] + [self.meet(own, bits) for bits in (1, 2, 3)]

    def scatter(self, far, near_of):
        sent = jnp.bfloat16
        cut = far.shape[0] // 2
        low_part = self.meet(far[:cut], 1)
        high_part = self.meet(far[cut:], 2)
        own, first, second = near_of()
        first = jnp.concatenate([first[:cut], first[cut:] + high_part], 0).astype(sent)
        second = jnp.concatenate([second[:cut] + low_part, second[cut:]], 0).astype(sent)
        from_first = self.meet(first, 1)
        from_second = self.meet(second, 2)
        total = own + from_first.astype(jnp.float32) + from_second.astype(jnp.float32)
        return total, (first, second)

    def scatter_small(self, terms):
        def pick(j):
            return lax.dynamic_index_in_dim(terms, self.place ^ j, 0, keepdims=False)

        passed = pick(2) + self.meet(pick(3), 1)
        return pick(0) + self.meet(pick(1), 1) + self.meet(passed, 2)

    def ordered(self, slots, axis):
        extent = slots[0].shape[axis]
        shape = list(slots[0].shape)
        shape[axis] = 4 * extent
        whole = jnp.zeros(shape, slots[0].dtype)
        for j in range(4):
            whole = lax.dynamic_update_slice_in_dim(
                whole, slots[j], (self.place ^ j) * extent, axis
            )
        return whole


def twin(block):
    return lax.ppermute(block, "wide", meeting(1, 1, lax.axis_size("wide")))


def custom_mesh():
    return lax.axis_size("wide") == 8 and lax.axis_size("tensor") == 4


def after(values, earlier):
    return lax.optimization_barrier((values, earlier))[0]


def relative_columns(values):
    if not custom_mesh():
        return values
    extent = values.shape[-1] // 8
    place = lax.axis_index("wide")
    blocks = [
        lax.dynamic_slice_in_dim(values, (place ^ m) * extent, extent, values.ndim - 1)
        for m in range(8)
    ]
    return jnp.concatenate(blocks, -1)


def wide_gather(own):
    if not custom_mesh():
        whole = lax.all_gather(own, "wide", axis=0, tiled=True)
        return whole, whole
    slots = Square("wide", 2).gather(own)
    pairs = []
    for slot in slots:
        pairs += [slot, twin(slot)]
    return jnp.concatenate(pairs, 0), slots[3]


def wide_scatter(grad, earlier=None):
    grad = grad.astype(jnp.bfloat16)
    if not custom_mesh():
        total = lax.psum_scatter(grad, "wide", scatter_dimension=0, tiled=True).astype(jnp.float32)
        return total, total, total
    terms = grad.reshape(4, 2, grad.shape[0] // 8, -1)
    others = terms[:, 1]
    if earlier is not None:
        others = after(others, earlier)
    arrived = twin(others)

    def term_of(j):
        return terms[j, 0].astype(jnp.float32) + arrived[j].astype(jnp.float32)

    far = term_of(3).astype(jnp.bfloat16)
    total, passed_on = Square("wide", 2).scatter(far, lambda: [term_of(j) for j in range(3)])
    return total, far, passed_on


def rows_gather(values):
    if not custom_mesh():
        return lax.all_gather(values, "tensor", axis=0, tiled=True)
    square = Square("tensor", 1)
    return jnp.concatenate(square.gather(values), 0)


def relative_rows(values, local_rows):
    if not custom_mesh():
        return values
    place = lax.axis_index("tensor")
    return jnp.concatenate(
        [lax.dynamic_slice_in_dim(values, (place ^ j) * local_rows, local_rows, 0) for j in range(4)],
        0,
    )


def prompt_start(prompt_rows):
    if not custom_mesh():
        return jnp.int32(0)
    return lax.axis_index("tensor") // 2 * prompt_rows


def rows_scatter(term_fn, local_rows, earlier=None):
    if not custom_mesh():
        total = lax.psum_scatter(
            term_fn(0, local_rows * lax.axis_size("tensor"), None).astype(jnp.bfloat16),
            "tensor",
            scatter_dimension=0,
            tiled=True,
        ).astype(jnp.float32)
        return total, total, (term_fn(0, local_rows * lax.axis_size("tensor"), None),)
    far = term_fn(3 * local_rows, local_rows, None).astype(jnp.bfloat16)
    if earlier is not None:
        far = after(far, earlier)

    def near_of():
        near = term_fn(0, 3 * local_rows, far)
        shares.append(near)
        return [near[j * local_rows : (j + 1) * local_rows] for j in range(3)]

    shares = []
    total, passed_on = Square("tensor", 1).scatter(far, near_of)
    return total, passed_on, (shares[0], far)


def gains_gather(gains):
    if not custom_mesh():
        whole = lax.all_gather(gains, ("wide", "tensor"), axis=1, tiled=True)
        return whole, whole
    square = Square("tensor", 1)
    lanes = square.ordered(square.gather_small(gains[None]), 0)
    pair = jnp.stack([lanes, twin(lanes)])[None]
    whole = jnp.concatenate(Square("wide", 2).gather_small(pair), 0)
    return jnp.moveaxis(whole, 3, 0).reshape(gains.shape[0], -1), lanes


def gain_scatter(part):
    if not custom_mesh():
        return lax.psum_scatter(part, ("wide", "tensor"), scatter_dimension=0, tiled=True)
    terms = part.reshape(4, 2, 4, -1)
    kept = part.shape[1]
    terms = terms[:, 0] + twin(terms[:, 1])
    passed = terms[2] + Square("wide", 2).meet(terms[3], 1)
    chips = Square("wide", 2)
    terms = terms[0] + chips.meet(terms[1], 1) + chips.meet(passed, 2)
    return Square("tensor", 1).scatter_small(terms).reshape(-1, kept)


def rows_of(values, first_row, num_rows, earlier):
    rows = values[first_row : first_row + num_rows]
    return rows if earlier is None else after(rows, earlier)


def rope_kernel(v_ref, cos_ref, sin_ref, o_ref, *, turned_heads):
    values = v_ref[...]
    half_dim = values.shape[1] // 2
    lane = lax.broadcasted_iota(jnp.int32, values.shape, 1)
    turned = pltpu.roll(values, half_dim, 1)
    turned = jnp.where(lane < half_dim, -turned, turned)
    rotated = values * cos_ref[...] + turned * sin_ref[...]
    plain = pl.program_id(0) >= turned_heads
    o_ref[...] = jnp.where(plain, values, rotated).astype(jnp.bfloat16)


def rope(values, tables, turned_heads, head_dim):
    rows = values.shape[0]
    block = pl.BlockSpec((rows, head_dim), lambda h: (0, h))
    table = pl.BlockSpec((rows, head_dim), lambda h: (0, 0))

    def kernel(*refs):
        rope_kernel(*refs, turned_heads=turned_heads)

    return pl.pallas_call(
        kernel,
        grid=(values.shape[1] // head_dim,),
        in_specs=[block, table, table],
        out_specs=block,
        out_shape=jax.ShapeDtypeStruct(values.shape, jnp.bfloat16),
    )(values, *tables)


def column_scores(q_ref, k_ref, q_seg, q_pos, k_seg, k_pos, scale):
    scores = dot_back(k_ref[...], q_ref[...]) * scale
    allowed = ((k_seg[...] == 0) | (k_seg[...] == q_seg[...])) & (k_pos[...] <= q_pos[...])
    scores = jnp.where(allowed, scores, masked_score)
    exps = jnp.exp(scores - jnp.max(scores, axis=0, keepdims=True))
    return exps * (1.0 / jnp.sum(exps, axis=0, keepdims=True))


def attend_kernel(q_ref, k_ref, vt_ref, q_seg, q_pos, k_seg, k_pos, o_ref, *, scale):
    probs = column_scores(q_ref, k_ref, q_seg, q_pos, k_seg, k_pos, scale).astype(jnp.bfloat16)
    columns = jnp.dot(vt_ref[...], probs, preferred_element_type=jnp.float32)
    o_ref[...] = columns.T.astype(jnp.bfloat16)


def attend_back_kernel(
    q_ref, k_ref, kt_ref, v_ref, d_ref, cos_ref, sin_ref, q_seg, q_pos, k_seg, k_pos,
    dq_ref, dk_ref, dv_ref, *, scale,
):
    probs = column_scores(q_ref, k_ref, q_seg, q_pos, k_seg, k_pos, scale)
    d_probs = dot_back(v_ref[...], d_ref[...])
    term = jnp.sum(probs * d_probs, axis=0, keepdims=True)
    d_scores = (probs * (d_probs - term) * scale).astype(jnp.bfloat16)
    d_query = jnp.dot(kt_ref[...], d_scores, preferred_element_type=jnp.float32).T
    half_dim = d_query.shape[1] // 2
    lane = lax.broadcasted_iota(jnp.int32, d_query.shape, 1)
    turned = pltpu.roll(d_query, half_dim, 1)
    turned = jnp.where(lane < half_dim, -turned, turned)
    dq_ref[...] = (d_query * cos_ref[...] - turned * sin_ref[...]).astype(jnp.bfloat16)
    dk_part = jnp.dot(d_scores, q_ref[...], preferred_element_type=jnp.float32)
    dv_part = jnp.dot(
        probs.astype(jnp.bfloat16), d_ref[...], preferred_element_type=jnp.float32
    )
    first = (pl.program_id(1) == 0) & (pl.program_id(2) == 0)

    @pl.when(first)
    def _():
        dk_ref[...] = dk_part
        dv_ref[...] = dv_part

    @pl.when(jnp.logical_not(first))
    def _():
        dk_ref[...] += dk_part
        dv_ref[...] += dv_part


def attend_specs(block_rows, key_count, group_size, head_dim):
    def of_query(g, h, b):
        return (b, g * group_size + h)

    return dict(
        query=pl.BlockSpec((block_rows, head_dim), of_query),
        key=pl.BlockSpec((key_count, head_dim), lambda g, h, b: (0, g)),
        turned=pl.BlockSpec((head_dim, key_count), lambda g, h, b: (g, 0)),
        table=pl.BlockSpec((block_rows, head_dim), lambda g, h, b: (b, 0)),
        q_meta=pl.BlockSpec((1, block_rows), lambda g, h, b: (0, b)),
        k_meta=pl.BlockSpec((key_count, 1), lambda g, h, b: (0, 0)),
    )


def attend_forward(query, key, value, metas, head_dim, block_rows, scale):
    row_count, key_count = query.shape[0], key.shape[0]
    kv_heads = key.shape[1] // head_dim
    group_size = query.shape[1] // head_dim // kv_heads
    sp = attend_specs(block_rows, key_count, group_size, head_dim)

    def kernel(*refs):
        attend_kernel(*refs, scale=scale)

    return pl.pallas_call(
        kernel,
        grid=(kv_heads, group_size, row_count // block_rows),
        in_specs=[sp["query"], sp["key"], sp["turned"]] + [sp["q_meta"]] * 2 + [sp["k_meta"]] * 2,
        out_specs=sp["query"],
        out_shape=jax.ShapeDtypeStruct(query.shape, jnp.bfloat16),
    )(query, key, value.T, *metas)


def attend_backward(query, key, value, d_out, tables, metas, head_dim, block_rows, scale):
    row_count, key_count = query.shape[0], key.shape[0]
    kv_heads = key.shape[1] // head_dim
    group_size = query.shape[1] // head_dim // kv_heads
    sp = attend_specs(block_rows, key_count, group_size, head_dim)

    def kernel(*refs):
        attend_back_kernel(*refs, scale=scale)

    return pl.pallas_call(
        kernel,
        grid=(kv_heads, group_size, row_count // block_rows),
        in_specs=[sp["query"], sp["key"], sp["turned"], sp["key"], sp["query"]]
        + [sp["table"]] * 2
        + [sp["q_meta"]] * 2
        + [sp["k_meta"]] * 2,
        out_specs=[sp["query"], sp["key"], sp["key"]],
        out_shape=[
            jax.ShapeDtypeStruct(query.shape, jnp.bfloat16),
            jax.ShapeDtypeStruct(key.shape, jnp.float32),
            jax.ShapeDtypeStruct(key.shape, jnp.float32),
        ],
    )(query, key, key.T, value, d_out, *tables, *metas)


def on_device(
    layer_input,
    lengths,
    gain_attn,
    w_query,
    w_key,
    w_value,
    w_out,
    gain_ffn,
    w_gate,
    w_up,
    w_down,
    cotangent,
):
    tensor_count = lax.axis_size("tensor")
    local_rows = layer_input.shape[0]
    row_count = local_rows * tensor_count
    prompt_rows = PROMPT // 2
    head_dim = HEAD_DIM
    query_heads = w_query.shape[1] // head_dim
    kv_heads = w_key.shape[1] // head_dim
    group_size = query_heads // kv_heads
    score_scale = head_dim ** (-0.5)
    block_rows = min(256, row_count)
    half_index = lax.axis_index("wide") % 2
    low_type = jnp.bfloat16
    query_cols, kv_cols = w_query.shape[1], w_key.shape[1]
    hidden_cols = w_gate.shape[1]
    gains, _ = gains_gather(jnp.stack([gain_attn, gain_ffn]))
    gain_one, gain_two = gains[0], gains[1]
    layer_input = relative_columns(layer_input)
    cotangent = relative_columns(cotangent)
    x_low_all = rows_gather(layer_input)
    attn_own = jnp.concatenate([w_query, w_key, w_value, w_out.T], 1).astype(low_type)
    ffn_own = jnp.concatenate([w_gate, w_up, w_down.T], 1).astype(low_type)
    attn_wide, attn_far = wide_gather(attn_own)
    qkv_cols = query_cols + 2 * kv_cols
    qkv_wide, out_wide = attn_wide[:, :qkv_cols], attn_wide[:, qkv_cols:]
    ffn_wide, _ = wide_gather(after(ffn_own, attn_far))
    gate_up_wide, down_wide = ffn_wide[:, : 2 * hidden_cols], ffn_wide[:, 2 * hidden_cols :]
    cot_all = rows_gather(after(cotangent, x_low_all))
    x_float = layer_input.astype(jnp.float32)
    inv_one = lax.rsqrt(jnp.mean(x_float * x_float, axis=-1, keepdims=True) + norm_eps)
    normed_one = x_float * inv_one
    x_all = x_low_all.astype(jnp.float32)
    normed_all = x_all * lax.rsqrt(jnp.mean(x_all * x_all, axis=-1, keepdims=True) + norm_eps)
    h_one_all = (normed_all * gain_one).astype(jnp.bfloat16)
    qkv_raw = jnp.dot(h_one_all, qkv_wide, preferred_element_type=jnp.float32)
    segment, position = layout(lengths[0], half_index, row_count, prompt_rows)
    segment = relative_rows(segment, local_rows)
    position = relative_rows(position, local_rows)
    prompt_at = prompt_start(prompt_rows)
    cosine, sine_part = rope_tables(position, head_dim)
    tables = (cosine, sine_part)
    qkv_low = rope(qkv_raw, tables, query_heads + kv_heads, head_dim)
    query_rot, kv_low = qkv_low[:, :query_cols], qkv_low[:, query_cols:]
    far_kv = swapped(
        lax.dynamic_slice_in_dim(kv_low, prompt_at, prompt_rows, 0), "wide", 0
    )
    kv_all = jnp.concatenate([far_kv, kv_low], 0)
    key_all, value_all = kv_all[:, :kv_cols], kv_all[:, kv_cols:]
    own_prompt = lax.dynamic_slice_in_dim(position, prompt_at, prompt_rows, 0)
    far_position = own_prompt + (1 - 2 * half_index) * prompt_rows
    key_segment = jnp.concatenate([jnp.zeros((prompt_rows,), jnp.int32), segment])
    key_position = jnp.concatenate([far_position, position])
    span = group_size * head_dim
    metas = (segment[None], position[None], key_segment[:, None], key_position[:, None])
    head_query = [query_rot[:, g * span : (g + 1) * span] for g in range(kv_heads)]
    head_key = [key_all[:, g * head_dim : (g + 1) * head_dim] for g in range(kv_heads)]
    head_value = [value_all[:, g * head_dim : (g + 1) * head_dim] for g in range(kv_heads)]
    attn_parts = []
    for g in range(kv_heads):
        attn_parts.append(
            attend_forward(
                head_query[g],
                head_key[g],
                head_value[g],
                metas,
                head_dim,
                block_rows,
                score_scale,
            )
        )
    attn_low = jnp.concatenate(attn_parts, 1)

    def attn_term(first_row, num_rows, earlier):
        return dot_back(rows_of(attn_low, first_row, num_rows, earlier), out_wide)

    attn_sum, _, _ = rows_scatter(attn_term, local_rows, cot_all)
    x_mid = x_float + attn_sum
    inv_two = lax.rsqrt(jnp.mean(x_mid * x_mid, axis=-1, keepdims=True) + norm_eps)
    normed_two = x_mid * inv_two
    h_two = (normed_two * gain_two).astype(jnp.bfloat16)
    h_two_all = rows_gather(h_two)
    gate_up_val = jnp.dot(h_two_all, gate_up_wide, preferred_element_type=jnp.float32)
    gate_val = gate_up_val[:, :hidden_cols]
    up_val = gate_up_val[:, hidden_cols:]
    gate_sig = jax.nn.sigmoid(gate_val)
    hidden_low = (gate_val * gate_sig * up_val).astype(jnp.bfloat16)

    cot_float = cotangent.astype(jnp.float32)
    d_hidden = jnp.dot(cot_all, down_wide, preferred_element_type=jnp.float32)
    d_up = (d_hidden * gate_val * gate_sig).astype(jnp.bfloat16)
    d_gate = (d_hidden * up_val * gate_sig * (1.0 + gate_val * (1.0 - gate_sig))).astype(
        jnp.bfloat16
    )
    d_gate_up = jnp.concatenate([d_gate, d_up], 1)

    def ffn_back_term(first_row, num_rows, earlier):
        return dot_back(rows_of(d_gate_up, first_row, num_rows, earlier), gate_up_wide)

    d_h_two, passed_on, _ = rows_scatter(ffn_back_term, local_rows)
    d_gate_up_late, hidden_late = after((d_gate_up, hidden_low), passed_on)
    grad_gate_up = dot_rows(h_two_all, d_gate_up_late)
    grad_down = dot_rows(cot_all, hidden_late)
    gain_two_part = jnp.sum(d_h_two * normed_two, axis=0)
    e_two = d_h_two * gain_two
    d_mid = cot_float + inv_two * (
        e_two - normed_two * jnp.mean(e_two * normed_two, axis=-1, keepdims=True)
    )
    d_mid_all = rows_gather(d_mid.astype(jnp.bfloat16))

    def ffn_term(first_row, num_rows, earlier):
        return dot_back(rows_of(hidden_late, first_row, num_rows, earlier), down_wide)

    ffn_sum, _, _ = rows_scatter(ffn_term, local_rows, d_mid_all)
    output = (x_mid + ffn_sum).astype(jnp.bfloat16)
    grad_out = dot_rows(d_mid_all, attn_low)
    d_attended = jnp.dot(
        d_mid_all, out_wide, preferred_element_type=jnp.float32
    ).astype(jnp.bfloat16)
    grad_gate_up, _, _ = wide_scatter(grad_gate_up)
    grad_down, _, _ = wide_scatter(grad_down)
    grad_out, _, _ = wide_scatter(grad_out)
    back = []
    for g in range(kv_heads):
        d_head = d_attended[:, g * span : (g + 1) * span]
        if g:
            d_head = after(d_head, back[g - 1][0])
        back.append(
            attend_backward(
                head_query[g],
                head_key[g],
                head_value[g],
                d_head,
                tables,
                metas,
                head_dim,
                block_rows,
                score_scale,
            )
        )
    d_query_low = jnp.concatenate([part[0] for part in back], 1)
    key_grad = jnp.concatenate([part[1] for part in back], 1)
    value_grad = jnp.concatenate([part[2] for part in back], 1)
    kv_grad = jnp.concatenate([key_grad, value_grad], 1)
    far_grad = swapped(kv_grad[:prompt_rows].astype(low_type), "wide", 0)
    own_grad = kv_grad[prompt_rows:]
    prompt_part = lax.dynamic_slice_in_dim(own_grad, prompt_at, prompt_rows, 0)
    own_grad = lax.dynamic_update_slice_in_dim(
        own_grad, prompt_part + far_grad.astype(jnp.float32), prompt_at, 0
    )
    d_kv_low = rope(own_grad, (cosine, -sine_part), kv_heads, head_dim)
    d_qkv_low = jnp.concatenate([d_query_low, d_kv_low], 1)

    def attn_back_term(first_row, num_rows, earlier):
        return dot_back(rows_of(d_qkv_low, first_row, num_rows, earlier), qkv_wide)

    d_h_one, passed_on, shares = rows_scatter(attn_back_term, local_rows)
    grad_qkv = dot_rows(h_one_all, after(d_qkv_low, passed_on))
    x_late, shares = after((x_low_all, shares), passed_on)
    x_late = x_late.astype(jnp.float32)
    normed_late = x_late * lax.rsqrt(jnp.mean(x_late * x_late, axis=-1, keepdims=True) + norm_eps)
    gain_one_part, first_row = 0.0, 0
    for share in shares:
        end_row = first_row + share.shape[0]
        gain_one_part += jnp.sum(share.astype(jnp.float32) * normed_late[first_row:end_row], axis=0)
        first_row = end_row
    e_one = d_h_one * gain_one
    input_grad = (
        d_mid
        + inv_one * (e_one - normed_one * jnp.mean(e_one * normed_one, axis=-1, keepdims=True))
    ).astype(jnp.bfloat16)
    grad_qkv, _, _ = wide_scatter(grad_qkv)
    grad_down, grad_out = grad_down.T, grad_out.T
    grad_gate, grad_up = grad_gate_up[:, :hidden_cols], grad_gate_up[:, hidden_cols:]
    grad_query = grad_qkv[:, :query_cols]
    grad_key = grad_qkv[:, query_cols : query_cols + kv_cols]
    grad_value = grad_qkv[:, query_cols + kv_cols :]
    gain_grads = gain_scatter(jnp.stack([gain_one_part, gain_two_part], 1))
    grad_gain_one, grad_gain_two = gain_grads[:, 0], gain_grads[:, 1]
    return (
        relative_columns(output),
        relative_columns(input_grad),
        grad_gain_one,
        grad_query,
        grad_key,
        grad_value,
        grad_out,
        grad_gain_two,
        grad_gate,
        grad_up,
        grad_down,
    )


def solution(mesh):
    placed = (
        P(("wide", "tensor"), None),
        P("wide", None),
        P(("wide", "tensor")),
        P("wide", "tensor"),
        P("wide", "tensor"),
        P("wide", "tensor"),
        P("tensor", "wide"),
        P(("wide", "tensor")),
        P("wide", "tensor"),
        P("wide", "tensor"),
        P("tensor", "wide"),
        P(("wide", "tensor"), None),
    )

    return jax.shard_map(
        on_device,
        mesh=mesh,
        in_specs=placed,
        out_specs=(
            P(("wide", "tensor"), None),
            P(("wide", "tensor"), None),
            P(("wide", "tensor")),
            P("wide", "tensor"),
            P("wide", "tensor"),
            P("wide", "tensor"),
            P("tensor", "wide"),
            P(("wide", "tensor")),
            P("wide", "tensor"),
            P("wide", "tensor"),
            P("tensor", "wide"),
        ),
        check_vma=False,
    )
```
